256 devices in a mesh: ctx: 64 (over z, y, core), head: 4 (over x).
Axes of the slice: x: 4, y: 4, z: 8, core: 2. Of those that a mesh axis runs over, the one named last changes fastest.
Arguments:
- query: bfloat16 [32768, 8192], P('ctx', 'head'), may hold values from -6 to 6
- key: bfloat16 [32768, 1024], P('ctx', 'head'), may hold values from -6 to 6
- value: bfloat16 [32768, 1024], P('ctx', 'head'), may hold values from -6 to 6
- attn_out: bfloat16 [32768, 8192], P('ctx', 'head'), may hold values from -6 to 6
- grad_out: bfloat16 [32768, 8192], P('ctx', 'head'), may hold values from -48 to 48
- log_norm: float32 [64, 32768], P('head', 'ctx')
- doc_bounds: int32 [40], replicated, may hold values from 0 to 32768, as said below
- local_pairs: int32 [2816, 2], P('ctx'), may hold values from -1 to 15, as said below
- ship_table: int32 [64, 2, 9], replicated, may hold values from -1 to 15, as said below
Outputs:
- grad_query: bfloat16 [32768, 8192], P('ctx', 'head')
- grad_key: bfloat16 [32768, 1024], P('ctx', 'head')
- grad_value: bfloat16 [32768, 1024], P('ctx', 'head')
The draws below stay inside these ranges and needn't reach their ends.
Inputs may be any that keep to these rules, and one draw needn't show every extreme that they name: `doc_bounds`: entry 0 is 0, entry 39 is 32768, entries rise strictly. No document is longer than 1280 tokens, and one is exactly that long. `local_pairs`: rows (q, w) of ctx index c: q is one of its 4 query blocks, w a block of its key window of 16 blocks, which begins 3 * 4 blocks before its first block. Live rows come first; the others are -1 in both columns. Together with ship_table every block pair whose blocks hold a query token and a key token of one document, the key not after the query, is named exactly once, and no other pair is named. `ship_table`: row (c, r): column 0 is a query block of ctx index c; the other 8 columns are blocks of c's key window, live first (at least one), -1 after. The pairs of a row are computed by the index of ctx that differs from c in bit number log2(64) - 1 - r.
All inputs are finite; a program needn't handle non-finite values.
Results may differ from the reference program's by a relative error of at most 0.006.
Values may be sent and summed in bfloat16 or wider, within the bound.
A program may use at most 192 MiB of HBM per device.

```python
import jax
import jax.numpy as jnp
from jax import lax

HEAD_DIM = 128
Q_HEADS = 64
KV_HEADS = 8
BLOCK = 128
DOC_BLOCKS = 10
SHIP_SLOTS = 8
ROUNDS = 2
SEQ = 32768
BLOCKS = 256
DEV_BLOCKS = 4
REACH = 3
PAIR_SLOTS = 44
N_CTX = 64


def doc_lengths(streams):
    groups = SEQ // (32 * BLOCK)
    longest_len = DOC_BLOCKS * BLOCK
    if groups == 1:
        swing = jax.random.randint(streams[0], (2,), 1 - 3 * BLOCK, 3 * BLOCK)
        return jnp.stack([6 * BLOCK + swing[0], 6 * BLOCK - swing[0], jnp.full((), longest_len, jnp.int32), 5 * BLOCK + swing[1], 5 * BLOCK - swing[1]]).astype(jnp.int32)
    middle = groups - 1
    kinds = jax.random.randint(streams[0], (middle,), 0, 2)
    swing = jax.random.randint(streams[1], (middle, 2), 1 - 3 * BLOCK, 3 * BLOCK)
    lift = jax.random.randint(streams[2], (middle,), 0, 2 * BLOCK)
    lower = jax.random.randint(streams[3], (middle,), 0, 3 * BLOCK)
    longest = jnp.full((middle,), longest_len, jnp.int32)
    long_kind = jnp.stack([6 * BLOCK + swing[:, 0], 6 * BLOCK - swing[:, 0], longest, 5 * BLOCK + swing[:, 1], 5 * BLOCK - swing[:, 1]], axis=1)
    even_kind = jnp.stack([5 * BLOCK + swing[:, 0], 5 * BLOCK - swing[:, 0], 8 * BLOCK + lift, 7 * BLOCK - lift + lower, 7 * BLOCK - lower], axis=1)
    inner = jnp.where(kinds[:, None] == 1, long_kind, even_kind).reshape(-1)
    flip = jax.random.randint(streams[4], (), 0, 2)
    lead = jnp.where(flip == 1, jnp.array([16 * BLOCK - longest_len, longest_len], jnp.int32), jnp.array([longest_len, 16 * BLOCK - longest_len], jnp.int32))
    tail_swing = jax.random.randint(streams[5], (), 1 - 2 * BLOCK, 2 * BLOCK)
    tail = jnp.stack([8 * BLOCK + tail_swing, 8 * BLOCK - tail_swing])
    return jnp.concatenate([lead, inner, tail]).astype(jnp.int32)


def doc_plan(key):
    base = jax.random.fold_in(key, 4242)
    streams = jax.random.split(base, 8)
    lengths = doc_lengths(streams)
    bounds = jnp.concatenate([jnp.zeros((1,), jnp.int32), jnp.cumsum(lengths).astype(jnp.int32)])
    block_ids = jnp.arange(BLOCKS, dtype=jnp.int32)
    doc_first = jnp.sum((bounds[1:][None, :] <= (block_ids * BLOCK)[:, None]).astype(jnp.int32), axis=1)
    low = (bounds[doc_first] // BLOCK).reshape(N_CTX, DEV_BLOCKS)
    top = block_ids.reshape(N_CTX, DEV_BLOCKS)
    devices = jnp.arange(N_CTX, dtype=jnp.int32)
    load = jnp.sum(top - low + 1, axis=1)
    levels = N_CTX.bit_length() - 1
    window_first = (devices - REACH) * DEV_BLOCKS
    own_ids = jnp.arange(DEV_BLOCKS, dtype=jnp.int32)
    slot_ids = jnp.arange(SHIP_SLOTS, dtype=jnp.int32)
    table_rows = []
    for section in range(ROUNDS):
        partner = jnp.bitwise_xor(devices, 1 << levels - 1 - section)
        remaining = top - low + 1
        ranking = remaining * DEV_BLOCKS + (DEV_BLOCKS - 1 - own_ids)[None, :]
        chosen = jnp.argmax(ranking, axis=1).astype(jnp.int32)
        pick = (own_ids[None, :] == chosen[:, None]).astype(jnp.int32)
        rem_chosen = jnp.sum(remaining * pick, axis=1)
        low_chosen = jnp.sum(low * pick, axis=1)
        moved = jnp.clip((load - load[partner]) // 2, 1, SHIP_SLOTS)
        moved = jnp.minimum(moved, rem_chosen)
        slots = jnp.where(slot_ids[None, :] < moved[:, None], low_chosen[:, None] + slot_ids[None, :] - window_first[:, None], -1)
        leader = jnp.where(moved > 0, chosen, -1)
        table_rows.append(jnp.concatenate([leader[:, None], slots], axis=1))
        low = low + pick * moved[:, None]
        load = load - moved + moved[partner]
    table = jnp.stack(table_rows, axis=1).astype(jnp.int32)
    spans = jnp.arange(DOC_BLOCKS + 1, dtype=jnp.int32)
    kv_blocks = low[:, :, None] + spans[None, None, :]
    live = (kv_blocks <= top[:, :, None]).reshape(N_CTX, PAIR_SLOTS)
    query_col = jnp.broadcast_to(own_ids[None, :, None], kv_blocks.shape).reshape(N_CTX, PAIR_SLOTS)
    window_col = (kv_blocks - window_first[:, None, None]).reshape(N_CTX, PAIR_SLOTS)
    ranking = (1 - live.astype(jnp.int32)) * PAIR_SLOTS + jnp.arange(PAIR_SLOTS, dtype=jnp.int32)[None, :]
    order = jnp.argsort(ranking, axis=1)
    live = jnp.take_along_axis(live, order, axis=1)
    query_col = jnp.where(live, jnp.take_along_axis(query_col, order, axis=1), -1)
    window_col = jnp.where(live, jnp.take_along_axis(window_col, order, axis=1), -1)
    pairs = jnp.stack([query_col, window_col], axis=2).reshape(N_CTX * PAIR_SLOTS, 2).astype(jnp.int32)
    return (bounds, pairs, table)


def draw_doc_bounds(key, part):
    return doc_plan(key)[0]


def draw_local_pairs(key, part):
    return doc_plan(key)[1]


def draw_ship_table(key, part):
    return doc_plan(key)[2]


def draw_log_norm(key, part):
    bounds = doc_plan(key)[0]
    positions = jnp.arange(SEQ, dtype=jnp.int32)
    docs = jnp.sum((bounds[1:][None, :] <= positions[:, None]).astype(jnp.int32), axis=1)
    counts = positions - bounds[docs] + 1
    base_part = jnp.log(counts.astype(jnp.float32))
    noise_key = jax.random.fold_in(key, 977)
    noise = jax.random.uniform(noise_key, (Q_HEADS, SEQ), jnp.float32, -0.5, 0.5)
    return (base_part[None, :] + 0.5 + noise).astype(jnp.float32)


def block_scale(key, dims, pieces, low, largest):
    level, own = 1.0, jax.random.fold_in(key, 6)
    for dim, blocks in pieces:
        steps = jnp.exp(jax.random.uniform(jax.random.fold_in(own, dim), (blocks,), jnp.float32, low / len(pieces), largest / len(pieces)))
        level = level * jnp.repeat(steps, dims[dim] // blocks).reshape([-1 if axis == dim else 1 for axis in range(len(dims))])
    return level


def gaussian(key, dims, scale, bound, shards=(), held_as=jnp.bfloat16):
    values = jax.random.normal(key, dims, jnp.float32) * scale
    if len(shards) > 0:
        values = block_scale(key, dims, shards, -0.22, 0.18) * values
    return jnp.clip(values, min=-bound, max=bound).astype(held_as)


def setup_inputs(seed: int = 0) -> dict:
    seeds = jax.random.split(jax.random.key(seed), 10)
    query = gaussian(seeds[0], (SEQ, Q_HEADS * HEAD_DIM), 1.0, 6.0, ((0, 64), (1, 4)))
    key = gaussian(seeds[1], (SEQ, KV_HEADS * HEAD_DIM), 1.0, 6.0, ((0, 64), (1, 4)))
    value = gaussian(seeds[2], (SEQ, KV_HEADS * HEAD_DIM), 1.0, 6.0, ((0, 64), (1, 4)))
    attn_out = gaussian(seeds[3], (SEQ, Q_HEADS * HEAD_DIM), 1.0, 6.0, ((0, 64), (1, 4)))
    grad_out = gaussian(seeds[4], (SEQ, Q_HEADS * HEAD_DIM), 8.0, 48.0, ((0, 64), (1, 4)))
    log_norm = draw_log_norm(jax.random.fold_in(seeds[9], 71), 0)
    doc_bounds = draw_doc_bounds(jax.random.fold_in(seeds[9], 71), 0)
    local_pairs = draw_local_pairs(jax.random.fold_in(seeds[9], 71), 0)
    ship_table = draw_ship_table(jax.random.fold_in(seeds[9], 71), 0)
    return dict(query=query, key=key, value=value, attn_out=attn_out, grad_out=grad_out, log_norm=log_norm, doc_bounds=doc_bounds, local_pairs=local_pairs, ship_table=ship_table)


def doc_index(positions, doc_bounds):
    edges = doc_bounds[1:]
    return jnp.sum((edges[None, :] <= positions[:, None]).astype(jnp.int32), axis=1)


def listed_table(local_pairs, ship_table):
    width = BLOCKS + DOC_BLOCKS
    owners = jnp.arange(N_CTX * PAIR_SLOTS, dtype=jnp.int32) // PAIR_SLOTS
    live = local_pairs[:, 0] >= 0
    rows = jnp.where(live, owners * DEV_BLOCKS + local_pairs[:, 0], BLOCKS)
    cols = jnp.where(live, (owners - REACH) * DEV_BLOCKS + local_pairs[:, 1] + DOC_BLOCKS, 0)
    cols = jnp.clip(cols, 0, width - 1)
    table = jnp.zeros((BLOCKS + 1, width), jnp.int32).at[rows, cols].add(1)
    devices = jnp.arange(N_CTX, dtype=jnp.int32)[:, None, None]
    lead = ship_table[:, :, 0:1]
    slots = ship_table[:, :, 1:]
    live_ship = (slots >= 0) & (lead >= 0)
    rows_ship = jnp.where(live_ship, devices * DEV_BLOCKS + lead, BLOCKS).reshape(-1)
    cols_ship = jnp.where(live_ship, (devices - REACH) * DEV_BLOCKS + slots + DOC_BLOCKS, 0).reshape(-1)
    cols_ship = jnp.clip(cols_ship, 0, width - 1)
    table = table.at[rows_ship, cols_ship].add(1)
    return table[:BLOCKS] > 0


def reference(query, key, value, attn_out, grad_out, log_norm, doc_bounds, local_pairs, ship_table):
    group = Q_HEADS // KV_HEADS
    scale = HEAD_DIM ** -0.5
    window = (DOC_BLOCKS + 1) * BLOCK
    margin = DOC_BLOCKS * BLOCK
    listed = listed_table(local_pairs, ship_table)
    key_pad = jnp.concatenate([jnp.zeros((margin, KV_HEADS * HEAD_DIM), key.dtype), key], axis=0)
    value_pad = jnp.concatenate([jnp.zeros((margin, KV_HEADS * HEAD_DIM), value.dtype), value], axis=0)
    doc_of = doc_index(jnp.arange(SEQ, dtype=jnp.int32), doc_bounds)
    doc_pad = jnp.concatenate([jnp.full((margin,), -1, jnp.int32), doc_of], axis=0)
    offsets = jnp.arange(BLOCK, dtype=jnp.int32)
    spread = jnp.arange(window, dtype=jnp.int32)

    def step(carry, block):
        grad_keys, grad_values = carry
        start = block * BLOCK
        queries = lax.dynamic_slice_in_dim(query, start, BLOCK, 0).astype(jnp.float32).reshape(BLOCK, KV_HEADS, group, HEAD_DIM)
        outgrads = lax.dynamic_slice_in_dim(grad_out, start, BLOCK, 0).astype(jnp.float32).reshape(BLOCK, KV_HEADS, group, HEAD_DIM)
        outputs = lax.dynamic_slice_in_dim(attn_out, start, BLOCK, 0).astype(jnp.float32).reshape(BLOCK, KV_HEADS, group, HEAD_DIM)
        dots = jnp.sum(outgrads * outputs, axis=3).transpose(1, 2, 0)
        norms = lax.dynamic_slice_in_dim(log_norm, start, BLOCK, 1).reshape(KV_HEADS, group, BLOCK)
        keys = lax.dynamic_slice_in_dim(key_pad, start, window, 0).astype(jnp.float32).reshape(window, KV_HEADS, HEAD_DIM)
        values = lax.dynamic_slice_in_dim(value_pad, start, window, 0).astype(jnp.float32).reshape(window, KV_HEADS, HEAD_DIM)
        query_pos = start + offsets
        key_pos = start - margin + spread
        query_doc = lax.dynamic_slice_in_dim(doc_of, start, BLOCK, 0)
        key_doc = lax.dynamic_slice_in_dim(doc_pad, start, window, 0)
        blocks_ok = lax.dynamic_slice_in_dim(listed[block], block, DOC_BLOCKS + 1, 0)
        key_ok = jnp.repeat(blocks_ok, BLOCK, total_repeat_length=window)
        allowed = (key_pos[None, :] <= query_pos[:, None]) & (key_doc[None, :] == query_doc[:, None]) & key_ok[None, :]
        scores = jnp.einsum("qhgd,khd->hgqk", queries, keys) * scale
        weights = jnp.where(allowed[None, None], jnp.exp(scores - norms[..., None]), 0.0)
        weight_grads = jnp.einsum("qhgd,khd->hgqk", outgrads, values)
        score_grads = lax.optimization_barrier((weights * (weight_grads - dots[..., None])).astype(jnp.bfloat16)).astype(jnp.float32)
        weights_low = lax.optimization_barrier(weights.astype(jnp.bfloat16)).astype(jnp.float32)
        grad_rows = jnp.einsum("hgqk,khd->qhgd", score_grads, keys) * scale
        part_keys = jnp.einsum("hgqk,qhgd->khd", score_grads, queries) * scale
        part_values = jnp.einsum("hgqk,qhgd->khd", weights_low, outgrads)
        grad_keys = lax.dynamic_update_slice_in_dim(grad_keys, lax.dynamic_slice_in_dim(grad_keys, start, window, 0) + part_keys.reshape(window, KV_HEADS * HEAD_DIM), start, 0)
        grad_values = lax.dynamic_update_slice_in_dim(grad_values, lax.dynamic_slice_in_dim(grad_values, start, window, 0) + part_values.reshape(window, KV_HEADS * HEAD_DIM), start, 0)
        return (grad_keys, grad_values), grad_rows.reshape(BLOCK, Q_HEADS * HEAD_DIM).astype(jnp.bfloat16)

    empty = jnp.zeros((SEQ + margin, KV_HEADS * HEAD_DIM), jnp.float32)
    (grad_keys, grad_values), grad_rows = lax.scan(step, (empty, empty), jnp.arange(BLOCKS, dtype=jnp.int32))
    grad_query = grad_rows.reshape(SEQ, Q_HEADS * HEAD_DIM)
    return (grad_query, grad_keys[margin:].astype(jnp.bfloat16), grad_values[margin:].astype(jnp.bfloat16))
```

```python
import functools
import jax
import jax.numpy as jnp
from jax import lax
from jax.experimental import pallas as pl
from jax.experimental.pallas import tpu as pltpu
from jax.sharding import PartitionSpec as P

HEAD_DIM = 128
BLOCK = 128

NT = (((1,), (1,)), ((), ()))
TN = (((0,), (0,)), ((), ()))


def pair_kernel(pairs_ref, count_ref, q_ref, do_ref, norm_ref, delta_ref, qdoc_ref, qpos_ref,
                kdoc_ref, kpos_ref, kv_ref, dq_ref, dkv_ref):
    dq_ref[...] = jnp.zeros(dq_ref.shape, jnp.float32)
    dkv_ref[...] = jnp.zeros(dkv_ref.shape, jnp.float32)
    heads = norm_ref.shape[0]
    kv_features = kv_ref.shape[1] // 2
    kv_heads = kv_features // HEAD_DIM
    group = heads // kv_heads
    scale = HEAD_DIM ** (-0.5)

    def body(i, carry):
        qb = jnp.maximum(pairs_ref[2 * i], 0)
        kb = jnp.maximum(pairs_ref[2 * i + 1], 0)
        qrow = pl.multiple_of(qb * BLOCK, BLOCK)
        krow = pl.multiple_of(kb * BLOCK, BLOCK)
        qdoc = qdoc_ref[pl.ds(qb, 1), :]
        qpos = qpos_ref[pl.ds(qb, 1), :]
        kdoc = kdoc_ref[pl.ds(krow, BLOCK), :]
        kpos = kpos_ref[pl.ds(krow, BLOCK), :]
        allowed = (kdoc == qdoc) & (kpos <= qpos)
        for g in range(kv_heads):
            k = kv_ref[pl.ds(krow, BLOCK), pl.ds(g * HEAD_DIM, HEAD_DIM)]
            v = kv_ref[pl.ds(krow, BLOCK), pl.ds(kv_features + g * HEAD_DIM, HEAD_DIM)]
            dk = jnp.zeros((BLOCK, HEAD_DIM), jnp.float32)
            dv = jnp.zeros((BLOCK, HEAD_DIM), jnp.float32)
            for j in range(group):
                h = g * group + j
                cols = pl.ds(h * HEAD_DIM, HEAD_DIM)
                q = q_ref[pl.ds(qrow, BLOCK), cols]
                do = do_ref[pl.ds(qrow, BLOCK), cols]
                norm = norm_ref[pl.ds(h, 1), pl.ds(qrow, BLOCK)]
                dl = delta_ref[pl.ds(h, 1), pl.ds(qrow, BLOCK)]
                scores = lax.dot_general(k, q, NT, preferred_element_type=jnp.float32) * scale
                weights = jnp.where(allowed, jnp.exp(scores - norm), 0.0)
                weight_grads = lax.dot_general(v, do, NT, preferred_element_type=jnp.float32)
                score_grads = (weights * (weight_grads - dl)).astype(jnp.bfloat16)
                weights_low = weights.astype(jnp.bfloat16)
                dv = dv + jnp.dot(weights_low, do, preferred_element_type=jnp.float32)
                dk = dk + jnp.dot(score_grads, q, preferred_element_type=jnp.float32)
                part_query = lax.dot_general(score_grads, k, TN, preferred_element_type=jnp.float32)
                dq_ref[pl.ds(qrow, BLOCK), cols] += part_query * scale
            dkv_ref[pl.ds(krow, BLOCK), pl.ds(g * HEAD_DIM, HEAD_DIM)] += dk * scale
            dkv_ref[pl.ds(krow, BLOCK), pl.ds(kv_features + g * HEAD_DIM, HEAD_DIM)] += dv
        return carry

    lax.fori_loop(0, count_ref[0], body, 0)


def run_pairs(pairs, count, queries, outgrads, norms, deltas, query_pos, keyval, key_pos, doc_bounds):
    q_doc = doc_index(query_pos, doc_bounds)
    k_doc = doc_index(key_pos, doc_bounds)
    tokens, features = queries.shape
    window, both = keyval.shape
    vmem = pltpu.MemorySpace.VMEM
    smem = pltpu.MemorySpace.SMEM
    args = (
        pairs.reshape(-1).astype(jnp.int32),
        jnp.reshape(count, (1,)).astype(jnp.int32),
        queries, outgrads, norms, deltas,
        q_doc, query_pos,
        k_doc.reshape(window, 1), key_pos.reshape(window, 1),
        keyval,
    )
    specs = [pl.BlockSpec(memory_space=smem)] * 2 + [pl.BlockSpec(memory_space=vmem)] * 9
    return pl.pallas_call(
        pair_kernel,
        out_shape=(
            jax.ShapeDtypeStruct((tokens, features), jnp.float32),
            jax.ShapeDtypeStruct((window, both), jnp.float32),
        ),
        in_specs=specs,
        out_specs=(pl.BlockSpec(memory_space=vmem), pl.BlockSpec(memory_space=vmem)),
        compiler_params=pltpu.CompilerParams(vmem_limit_bytes=48 * 1024 * 1024),
    )(*args)


SHIP_SLOTS = 8
ROUNDS = 2
REACH = 3
WIN_BLOCKS = 16


def shifted(shard, axis, by):
    length = lax.axis_size(axis)
    pairs = [(i, i + by) for i in range(length) if 0 <= i + by < length]
    return lax.ppermute(shard, axis, pairs)


def swapped(shard, axis, apart):
    return lax.ppermute(shard, axis, [(i, i ^ 1 << apart) for i in range(lax.axis_size(axis))])


def doc_index(positions, doc_bounds):
    flat = positions.reshape(-1)
    edges = doc_bounds[1:]
    counts = jnp.sum((edges[None, :] <= flat[:, None]).astype(jnp.int32), axis=1)
    return counts.reshape(positions.shape)


def local(query, key, value, attn_out, grad_out, log_norm, doc_bounds, local_pairs, ship_table):
    position = lax.axis_index("ctx")
    tokens, features = query.shape
    kv_features = key.shape[1]
    heads = log_norm.shape[0]
    own_blocks = tokens // BLOCK
    offsets = jnp.arange(BLOCK, dtype=jnp.int32)
    delta = jnp.einsum(
        "thd,thd->ht",
        grad_out.reshape(tokens, heads, HEAD_DIM),
        attn_out.reshape(tokens, heads, HEAD_DIM),
        preferred_element_type=jnp.float32,
    )
    own_keyval = jnp.concatenate([key, value], axis=1)
    pieces = []
    for hop in range(REACH, 0, -1):
        pieces.append(shifted(own_keyval, "ctx", hop))
    keyval_window = jnp.concatenate(pieces + [own_keyval], axis=0)
    first_block = position * own_blocks
    query_pos = (first_block + jnp.arange(own_blocks, dtype=jnp.int32))[:, None] * BLOCK + offsets
    window_first = first_block - REACH * own_blocks
    key_pos = (window_first * BLOCK + jnp.arange(WIN_BLOCKS * BLOCK, dtype=jnp.int32))
    local_count = jnp.sum((local_pairs[:, 0] >= 0).astype(jnp.int32))
    query_grads, keyval_grads = run_pairs(
        local_pairs, local_count, query, grad_out, log_norm, delta, query_pos,
        keyval_window, key_pos, doc_bounds,
    )
    query_grads = query_grads.reshape(own_blocks, BLOCK, features)
    keyval_grads = keyval_grads.reshape(WIN_BLOCKS, BLOCK, 2 * kv_features)
    queries = query.reshape(own_blocks, BLOCK, features)
    outgrads = grad_out.reshape(own_blocks, BLOCK, features)
    window_blocks = keyval_window.reshape(WIN_BLOCKS, BLOCK, 2 * kv_features)
    head_bits = lax.axis_size("head").bit_length() - 1
    all_bits = lax.axis_size(("ctx", "head")).bit_length() - 1
    slot_range = jnp.arange(SHIP_SLOTS, dtype=jnp.int32)
    for section in range(ROUNDS):
        my_row = ship_table[position, section]
        bit = all_bits - 1 - section
        partner = jnp.bitwise_xor(position, 1 << bit - head_bits)
        far_row = ship_table[partner, section]
        sent = jnp.maximum(my_row[0], 0)
        my_slots = jnp.maximum(my_row[1:], 0)
        sent_norms = lax.dynamic_slice_in_dim(log_norm, sent * BLOCK, BLOCK, 1)
        sent_delta = lax.dynamic_slice_in_dim(delta, sent * BLOCK, BLOCK, 1)
        got_norms, got_delta = swapped((sent_norms, sent_delta), ("ctx", "head"), bit)
        got_query, got_grad, got_keyval = swapped(
            (queries[sent], outgrads[sent], window_blocks[my_slots]), ("ctx", "head"), bit
        )
        far_count = jnp.sum((far_row[1:] >= 0).astype(jnp.int32))
        far_pairs = jnp.stack([jnp.zeros_like(slot_range), slot_range], axis=1)
        far_query_pos = ((partner * own_blocks + jnp.maximum(far_row[0], 0)) * BLOCK + offsets)[None]
        far_first = (partner - REACH) * own_blocks
        far_key_pos = (
            (far_first + jnp.maximum(far_row[1:], 0))[:, None] * BLOCK + offsets
        ).reshape(-1)
        back_query, back_keyval = run_pairs(
            far_pairs, far_count, got_query, got_grad, got_norms, got_delta, far_query_pos,
            got_keyval.reshape(SHIP_SLOTS * BLOCK, 2 * kv_features), far_key_pos, doc_bounds,
        )
        returned = swapped(
            (back_query, back_keyval.reshape(SHIP_SLOTS, BLOCK, 2 * kv_features)),
            ("ctx", "head"), bit,
        )
        query_grads = query_grads.at[sent].add(returned[0])
        keyval_grads = keyval_grads.at[my_slots].add(returned[1])
    segments = keyval_grads.reshape(REACH + 1, own_blocks * BLOCK, 2 * kv_features)
    own_grads = segments[REACH]
    for hop in range(1, REACH + 1):
        own_grads = own_grads + shifted(segments[REACH - hop], "ctx", -hop)
    grad_query = query_grads.reshape(tokens, features).astype(jnp.bfloat16)
    grad_key = own_grads[:, :kv_features].astype(jnp.bfloat16)
    grad_value = own_grads[:, kv_features:].astype(jnp.bfloat16)
    return (grad_query, grad_key, grad_value)


def solution(mesh):
    in_specs = (
        P("ctx", "head"),
        P("ctx", "head"),
        P("ctx", "head"),
        P("ctx", "head"),
        P("ctx", "head"),
        P("head", "ctx"),
        P(),
        P("ctx", None),
        P(),
    )
    out_specs = (P("ctx", "head"), P("ctx", "head"), P("ctx", "head"))
    return jax.shard_map(local, mesh=mesh, in_specs=in_specs, out_specs=out_specs, check_vma=False)
```

```python
import functools
import jax
import jax.numpy as jnp
from jax import lax
from jax.experimental import pallas as pl
from jax.experimental.pallas import tpu as pltpu
from jax.sharding import PartitionSpec as P

HEAD_DIM = 128
BLOCK = 128

NT = (((1,), (1,)), ((), ()))
TN = (((0,), (0,)), ((), ()))


def pair_kernel(pairs_ref, q_ref, do_ref, norm_ref, delta_ref, qdoc_ref, qpos_ref,
                kdoc_ref, kpos_ref, kv_ref, dq_ref, dkv_ref):
    dq_ref[...] = jnp.zeros(dq_ref.shape, jnp.float32)
    dkv_ref[...] = jnp.zeros(dkv_ref.shape, jnp.float32)
    heads = norm_ref.shape[0]
    kv_features = kv_ref.shape[1] // 2
    kv_heads = kv_features // HEAD_DIM
    group = heads // kv_heads
    scale = HEAD_DIM ** (-0.5)

    def body(i, carry):
        qb_raw = pairs_ref[2 * i]
        kb_raw = pairs_ref[2 * i + 1]
        pl.when((qb_raw >= 0) & (kb_raw >= 0))(lambda: one_pair(jnp.maximum(qb_raw, 0), jnp.maximum(kb_raw, 0)))
        return carry

    def one_pair(qb, kb):
        qrow = pl.multiple_of(qb * BLOCK, BLOCK)
        krow = pl.multiple_of(kb * BLOCK, BLOCK)
        qdoc = qdoc_ref[pl.ds(qb, 1), :]
        qpos = qpos_ref[pl.ds(qb, 1), :]
        kdoc = kdoc_ref[pl.ds(krow, BLOCK), :]
        kpos = kpos_ref[pl.ds(krow, BLOCK), :]
        allowed = (kdoc == qdoc) & (kpos <= qpos)
        for g in range(kv_heads):
            k = kv_ref[pl.ds(krow, BLOCK), pl.ds(g * HEAD_DIM, HEAD_DIM)]
            v = kv_ref[pl.ds(krow, BLOCK), pl.ds(kv_features + g * HEAD_DIM, HEAD_DIM)]
            dk = jnp.zeros((BLOCK, HEAD_DIM), jnp.float32)
            dv = jnp.zeros((BLOCK, HEAD_DIM), jnp.float32)
            for j in range(group):
                h = g * group + j
                cols = pl.ds(h * HEAD_DIM, HEAD_DIM)
                q = q_ref[pl.ds(qrow, BLOCK), cols]
                do = do_ref[pl.ds(qrow, BLOCK), cols]
                norm = norm_ref[pl.ds(h, 1), pl.ds(qrow, BLOCK)]
                dl = delta_ref[pl.ds(h, 1), pl.ds(qrow, BLOCK)]
                scores = lax.dot_general(k, q, NT, preferred_element_type=jnp.float32) * scale
                weights = jnp.where(allowed, jnp.exp(scores - norm), 0.0)
                weight_grads = lax.dot_general(v, do, NT, preferred_element_type=jnp.float32)
                score_grads = (weights * (weight_grads - dl)).astype(jnp.bfloat16)
                weights_low = weights.astype(jnp.bfloat16)
                dv = dv + jnp.dot(weights_low, do, preferred_element_type=jnp.float32)
                dk = dk + jnp.dot(score_grads, q, preferred_element_type=jnp.float32)
                part_query = lax.dot_general(score_grads, k, TN, preferred_element_type=jnp.float32)
                dq_ref[pl.ds(qrow, BLOCK), cols] += part_query * scale
            dkv_ref[pl.ds(krow, BLOCK), pl.ds(g * HEAD_DIM, HEAD_DIM)] += dk * scale
            dkv_ref[pl.ds(krow, BLOCK), pl.ds(kv_features + g * HEAD_DIM, HEAD_DIM)] += dv

    lax.fori_loop(0, pairs_ref.shape[0] // 2, body, 0)


def run_pairs(pairs, queries, outgrads, norms, deltas, query_pos, keyval, key_pos, doc_bounds):
    q_doc = doc_index(query_pos, doc_bounds)
    k_doc = doc_index(key_pos, doc_bounds)
    tokens, features = queries.shape
    window, both = keyval.shape
    vmem = pltpu.MemorySpace.VMEM
    smem = pltpu.MemorySpace.SMEM
    args = (
        pairs.reshape(-1).astype(jnp.int32),
        queries, outgrads, norms, deltas,
        q_doc, query_pos,
        k_doc.reshape(window, 1), key_pos.reshape(window, 1),
        keyval,
    )
    specs = [pl.BlockSpec(memory_space=smem)] + [pl.BlockSpec(memory_space=vmem)] * 9
    return pl.pallas_call(
        pair_kernel,
        out_shape=(
            jax.ShapeDtypeStruct((tokens, features), jnp.float32),
            jax.ShapeDtypeStruct((window, both), jnp.float32),
        ),
        in_specs=specs,
        out_specs=(pl.BlockSpec(memory_space=vmem), pl.BlockSpec(memory_space=vmem)),
        compiler_params=pltpu.CompilerParams(vmem_limit_bytes=48 * 1024 * 1024),
    )(*args)


REACH = 3
WIN_BLOCKS = 16


def shifted(shard, axis, by):
    length = lax.axis_size(axis)
    pairs = [(i, i + by) for i in range(length) if 0 <= i + by < length]
    return lax.ppermute(shard, axis, pairs)


def doc_index(positions, doc_bounds):
    flat = positions.reshape(-1)
    edges = doc_bounds[1:]
    counts = jnp.sum((edges[None, :] <= flat[:, None]).astype(jnp.int32), axis=1)
    return counts.reshape(positions.shape)


def local(query, key, value, attn_out, grad_out, log_norm, doc_bounds, local_pairs, ship_table):
    position = lax.axis_index("ctx")
    tokens, features = query.shape
    kv_features = key.shape[1]
    heads = log_norm.shape[0]
    own_blocks = tokens // BLOCK
    offsets = jnp.arange(BLOCK, dtype=jnp.int32)
    delta = jnp.einsum(
        "thd,thd->ht",
        grad_out.reshape(tokens, heads, HEAD_DIM),
        attn_out.reshape(tokens, heads, HEAD_DIM),
        preferred_element_type=jnp.float32,
    )
    own_keyval = jnp.concatenate([key, value], axis=1)
    pieces = []
    for hop in range(REACH, 0, -1):
        pieces.append(shifted(own_keyval, "ctx", hop))
    keyval_window = jnp.concatenate(pieces + [own_keyval], axis=0)
    first_block = position * own_blocks
    query_pos = (first_block + jnp.arange(own_blocks, dtype=jnp.int32))[:, None] * BLOCK + offsets
    window_first = first_block - REACH * own_blocks
    key_pos = (window_first * BLOCK + jnp.arange(WIN_BLOCKS * BLOCK, dtype=jnp.int32))
    own_ship = ship_table[position]
    ship_keys = own_ship[:, 1:]
    ship_queries = jnp.where(ship_keys >= 0, own_ship[:, :1], -1)
    ship_pairs = jnp.stack([ship_queries, ship_keys], axis=2).reshape(-1, 2)
    pairs = jnp.concatenate([local_pairs, ship_pairs], axis=0)
    query_grads, keyval_grads = run_pairs(
        pairs, query, grad_out, log_norm, delta, query_pos,
        keyval_window, key_pos, doc_bounds,
    )
    segments = keyval_grads.reshape(REACH + 1, own_blocks * BLOCK, 2 * kv_features)
    own_grads = segments[REACH]
    for hop in range(1, REACH + 1):
        own_grads = own_grads + shifted(segments[REACH - hop], "ctx", -hop)
    grad_query = query_grads.reshape(tokens, features).astype(jnp.bfloat16)
    grad_key = own_grads[:, :kv_features].astype(jnp.bfloat16)
    grad_value = own_grads[:, kv_features:].astype(jnp.bfloat16)
    return (grad_query, grad_key, grad_value)


def solution(mesh):
    in_specs = (
        P("ctx", "head"),
        P("ctx", "head"),
        P("ctx", "head"),
        P("ctx", "head"),
        P("ctx", "head"),
        P("head", "ctx"),
        P(),
        P("ctx", None),
        P(),
    )
    out_specs = (P("ctx", "head"), P("ctx", "head"), P("ctx", "head"))
    return jax.shard_map(local, mesh=mesh, in_specs=in_specs, out_specs=out_specs, check_vma=False)
```

```python
import functools
import jax
import jax.numpy as jnp
from jax import lax
from jax.experimental import pallas as pl
from jax.experimental.pallas import tpu as pltpu
from jax.sharding import PartitionSpec as P

HEAD_DIM = 128
BLOCK = 128

NT = (((1,), (1,)), ((), ()))
TN = (((0,), (0,)), ((), ()))


def pair_kernel(pairs_ref, q_ref, do_ref, norm_ref, delta_ref, qdoc_ref, qpos_ref,
                kdoc_ref, kpos_ref, kv_ref, dq_ref, dkv_ref):
    dq_ref[...] = jnp.zeros(dq_ref.shape, jnp.float32)
    dkv_ref[...] = jnp.zeros(dkv_ref.shape, jnp.float32)
    heads = norm_ref.shape[1] // BLOCK
    kv_features = kv_ref.shape[1] // 2
    kv_heads = kv_features // HEAD_DIM
    group = heads // kv_heads
    scale = HEAD_DIM ** (-0.5)

    def body(i, carry):
        qb_raw = pairs_ref[2 * i]
        kb_raw = pairs_ref[2 * i + 1]
        pl.when((qb_raw >= 0) & (kb_raw >= 0))(lambda: one_pair(jnp.maximum(qb_raw, 0), jnp.maximum(kb_raw, 0)))
        return carry

    def one_pair(qb, kb):
        qrow = pl.multiple_of(qb * BLOCK, BLOCK)
        krow = pl.multiple_of(kb * BLOCK, BLOCK)
        qdoc = qdoc_ref[pl.ds(qb, 1), :]
        qpos = qpos_ref[pl.ds(qb, 1), :]
        kdoc = kdoc_ref[pl.ds(krow, BLOCK), :]
        kpos = kpos_ref[pl.ds(krow, BLOCK), :]
        allowed = (kdoc == qdoc) & (kpos <= qpos)
        wide_allowed = jnp.concatenate([allowed] * group, axis=1)
        for g in range(kv_heads):
            k = kv_ref[pl.ds(krow, BLOCK), pl.ds(g * HEAD_DIM, HEAD_DIM)]
            v = kv_ref[pl.ds(krow, BLOCK), pl.ds(kv_features + g * HEAD_DIM, HEAD_DIM)]
            head_cols = [pl.ds((g * group + j) * HEAD_DIM, HEAD_DIM) for j in range(group)]
            q = jnp.concatenate([q_ref[pl.ds(qrow, BLOCK), c] for c in head_cols], axis=0)
            do = jnp.concatenate([do_ref[pl.ds(qrow, BLOCK), c] for c in head_cols], axis=0)
            group_cols = pl.ds(g * group * BLOCK, group * BLOCK)
            norm = norm_ref[pl.ds(qb, 1), group_cols]
            dl = delta_ref[pl.ds(qb, 1), group_cols]
            scores = lax.dot_general(k, q, NT, preferred_element_type=jnp.float32) * scale
            weights = jnp.where(wide_allowed, jnp.exp(scores - norm), 0.0)
            weight_grads = lax.dot_general(v, do, NT, preferred_element_type=jnp.float32)
            score_grads = (weights * (weight_grads - dl)).astype(jnp.bfloat16)
            weights_low = weights.astype(jnp.bfloat16)
            dv = jnp.dot(weights_low, do, preferred_element_type=jnp.float32)
            dk = jnp.dot(score_grads, q, preferred_element_type=jnp.float32)
            part_query = lax.dot_general(score_grads, k, TN, preferred_element_type=jnp.float32) * scale
            for j, c in enumerate(head_cols):
                dq_ref[pl.ds(qrow, BLOCK), c] += part_query[j * BLOCK:(j + 1) * BLOCK]
            dkv_ref[pl.ds(krow, BLOCK), pl.ds(g * HEAD_DIM, HEAD_DIM)] += dk * scale
            dkv_ref[pl.ds(krow, BLOCK), pl.ds(kv_features + g * HEAD_DIM, HEAD_DIM)] += dv

    lax.fori_loop(0, pairs_ref.shape[0] // 2, body, 0)


def run_pairs(pairs, queries, outgrads, norms, deltas, query_pos, keyval, key_pos, doc_bounds):
    q_doc = doc_index(query_pos, doc_bounds)
    k_doc = doc_index(key_pos, doc_bounds)
    tokens, features = queries.shape
    window, both = keyval.shape
    heads = norms.shape[0]
    blocks = tokens // BLOCK
    norms = norms.reshape(heads, blocks, BLOCK).transpose(1, 0, 2).reshape(blocks, heads * BLOCK)
    deltas = deltas.reshape(heads, blocks, BLOCK).transpose(1, 0, 2).reshape(blocks, heads * BLOCK)
    vmem = pltpu.MemorySpace.VMEM
    smem = pltpu.MemorySpace.SMEM
    args = (
        pairs.reshape(-1).astype(jnp.int32),
        queries, outgrads, norms, deltas,
        q_doc, query_pos,
        k_doc.reshape(window, 1), key_pos.reshape(window, 1),
        keyval,
    )
    specs = [pl.BlockSpec(memory_space=smem)] + [pl.BlockSpec(memory_space=vmem)] * 9
    return pl.pallas_call(
        pair_kernel,
        out_shape=(
            jax.ShapeDtypeStruct((tokens, features), jnp.float32),
            jax.ShapeDtypeStruct((window, both), jnp.float32),
        ),
        in_specs=specs,
        out_specs=(pl.BlockSpec(memory_space=vmem), pl.BlockSpec(memory_space=vmem)),
        compiler_params=pltpu.CompilerParams(vmem_limit_bytes=48 * 1024 * 1024),
    )(*args)


REACH = 3
WIN_BLOCKS = 16


def shifted(shard, axis, by):
    length = lax.axis_size(axis)
    pairs = [(i, i + by) for i in range(length) if 0 <= i + by < length]
    return lax.ppermute(shard, axis, pairs)


def doc_index(positions, doc_bounds):
    flat = positions.reshape(-1)
    edges = doc_bounds[1:]
    counts = jnp.sum((edges[None, :] <= flat[:, None]).astype(jnp.int32), axis=1)
    return counts.reshape(positions.shape)


def local(query, key, value, attn_out, grad_out, log_norm, doc_bounds, local_pairs, ship_table):
    position = lax.axis_index("ctx")
    tokens, features = query.shape
    kv_features = key.shape[1]
    heads = log_norm.shape[0]
    own_blocks = tokens // BLOCK
    offsets = jnp.arange(BLOCK, dtype=jnp.int32)
    delta = jnp.einsum(
        "thd,thd->ht",
        grad_out.reshape(tokens, heads, HEAD_DIM),
        attn_out.reshape(tokens, heads, HEAD_DIM),
        preferred_element_type=jnp.float32,
    )
    own_keyval = jnp.concatenate([key, value], axis=1)
    pieces = []
    for hop in range(REACH, 0, -1):
        pieces.append(shifted(own_keyval, "ctx", hop))
    keyval_window = jnp.concatenate(pieces + [own_keyval], axis=0)
    first_block = position * own_blocks
    query_pos = (first_block + jnp.arange(own_blocks, dtype=jnp.int32))[:, None] * BLOCK + offsets
    window_first = first_block - REACH * own_blocks
    key_pos = (window_first * BLOCK + jnp.arange(WIN_BLOCKS * BLOCK, dtype=jnp.int32))
    own_ship = ship_table[position]
    ship_keys = own_ship[:, 1:]
    ship_queries = jnp.where(ship_keys >= 0, own_ship[:, :1], -1)
    ship_pairs = jnp.stack([ship_queries, ship_keys], axis=2).reshape(-1, 2)
    pairs = jnp.concatenate([local_pairs, ship_pairs], axis=0)
    query_grads, keyval_grads = run_pairs(
        pairs, query, grad_out, log_norm, delta, query_pos,
        keyval_window, key_pos, doc_bounds,
    )
    segments = keyval_grads.reshape(REACH + 1, own_blocks * BLOCK, 2 * kv_features)
    own_grads = segments[REACH]
    for hop in range(1, REACH + 1):
        own_grads = own_grads + shifted(segments[REACH - hop], "ctx", -hop)
    grad_query = query_grads.reshape(tokens, features).astype(jnp.bfloat16)
    grad_key = own_grads[:, :kv_features].astype(jnp.bfloat16)
    grad_value = own_grads[:, kv_features:].astype(jnp.bfloat16)
    return (grad_query, grad_key, grad_value)


def solution(mesh):
    in_specs = (
        P("ctx", "head"),
        P("ctx", "head"),
        P("ctx", "head"),
        P("ctx", "head"),
        P("ctx", "head"),
        P("head", "ctx"),
        P(),
        P("ctx", None),
        P(),
    )
    out_specs = (P("ctx", "head"), P("ctx", "head"), P("ctx", "head"))
    return jax.shard_map(local, mesh=mesh, in_specs=in_specs, out_specs=out_specs, check_vma=False)
```

```python
import functools
import jax
import jax.numpy as jnp
from jax import lax
from jax.experimental import pallas as pl
from jax.experimental.pallas import tpu as pltpu
from jax.sharding import PartitionSpec as P

HEAD_DIM = 128
BLOCK = 128

NT = (((1,), (1,)), ((), ()))
TN = (((0,), (0,)), ((), ()))


def pair_kernel(pairs_ref, q_ref, do_ref, norm_ref, delta_ref, qdoc_ref, qpos_ref,
                kdoc_ref, kpos_ref, kv_ref, dq_ref, dkv_ref):
    dq_ref[...] = jnp.zeros(dq_ref.shape, jnp.float32)
    dkv_ref[...] = jnp.zeros(dkv_ref.shape, jnp.float32)
    heads = norm_ref.shape[1] // BLOCK
    kv_features = kv_ref.shape[1] // 2
    kv_heads = kv_features // HEAD_DIM
    group = heads // kv_heads
    scale = HEAD_DIM ** (-0.5)

    def body(i, carry):
        qb_raw = pairs_ref[2 * i]
        kb_raw = pairs_ref[2 * i + 1]
        pl.when((qb_raw >= 0) & (kb_raw >= 0))(lambda: one_pair(jnp.maximum(qb_raw, 0), jnp.maximum(kb_raw, 0)))
        return carry

    def one_pair(qb, kb):
        qrow = pl.multiple_of(qb * BLOCK, BLOCK)
        krow = pl.multiple_of(kb * BLOCK, BLOCK)
        qdoc = qdoc_ref[pl.ds(qb, 1), :]
        qpos = qpos_ref[pl.ds(qb, 1), :]
        kdoc = kdoc_ref[pl.ds(krow, BLOCK), :]
        kpos = kpos_ref[pl.ds(krow, BLOCK), :]
        allowed = (kdoc == qdoc) & (kpos <= qpos)
        wide_allowed = jnp.concatenate([allowed] * group, axis=1)
        for g in range(kv_heads):
            k = kv_ref[pl.ds(krow, BLOCK), pl.ds(g * HEAD_DIM, HEAD_DIM)]
            v = kv_ref[pl.ds(krow, BLOCK), pl.ds(kv_features + g * HEAD_DIM, HEAD_DIM)]
            head_cols = [pl.ds((g * group + j) * HEAD_DIM, HEAD_DIM) for j in range(group)]
            q = jnp.concatenate([q_ref[pl.ds(qrow, BLOCK), c] for c in head_cols], axis=0)
            do = jnp.concatenate([do_ref[pl.ds(qrow, BLOCK), c] for c in head_cols], axis=0)
            group_cols = pl.ds(g * group * BLOCK, group * BLOCK)
            norm = norm_ref[pl.ds(qb, 1), group_cols]
            dl = delta_ref[pl.ds(qb, 1), group_cols]
            scores = lax.dot_general(k, q, NT, preferred_element_type=jnp.float32) * scale
            weights = jnp.where(wide_allowed, jnp.exp(scores - norm), 0.0)
            weight_grads = lax.dot_general(v, do, NT, preferred_element_type=jnp.float32)
            score_grads = (weights * (weight_grads - dl)).astype(jnp.bfloat16)
            weights_low = weights.astype(jnp.bfloat16)
            dv = jnp.dot(weights_low, do, preferred_element_type=jnp.float32)
            dk = jnp.dot(score_grads, q, preferred_element_type=jnp.float32)
            part_query = lax.dot_general(score_grads, k, TN, preferred_element_type=jnp.float32) * scale
            for j, c in enumerate(head_cols):
                dq_ref[pl.ds(qrow, BLOCK), c] += part_query[j * BLOCK:(j + 1) * BLOCK]
            dkv_ref[pl.ds(krow, BLOCK), pl.ds(g * HEAD_DIM, HEAD_DIM)] += dk * scale
            dkv_ref[pl.ds(krow, BLOCK), pl.ds(kv_features + g * HEAD_DIM, HEAD_DIM)] += dv

    lax.fori_loop(0, pairs_ref.shape[0] // 2, body, 0)


def run_pairs(pairs, queries, outgrads, norms, deltas, query_pos, keyval, key_pos, doc_bounds):
    q_doc = doc_index(query_pos, doc_bounds)
    k_doc = doc_index(key_pos, doc_bounds)
    tokens, features = queries.shape
    window, both = keyval.shape
    heads = norms.shape[0]
    blocks = tokens // BLOCK
    norms = norms.reshape(heads, blocks, BLOCK).transpose(1, 0, 2).reshape(blocks, heads * BLOCK)
    deltas = deltas.reshape(heads, blocks, BLOCK).transpose(1, 0, 2).reshape(blocks, heads * BLOCK)
    vmem = pltpu.MemorySpace.VMEM
    smem = pltpu.MemorySpace.SMEM
    args = (
        pairs.reshape(-1).astype(jnp.int32),
        queries, outgrads, norms, deltas,
        q_doc, query_pos,
        k_doc.reshape(window, 1), key_pos.reshape(window, 1),
        keyval,
    )
    specs = [pl.BlockSpec(memory_space=smem)] + [pl.BlockSpec(memory_space=vmem)] * 9
    return pl.pallas_call(
        pair_kernel,
        out_shape=(
            jax.ShapeDtypeStruct((tokens, features), jnp.float32),
            jax.ShapeDtypeStruct((window, both), jnp.float32),
        ),
        in_specs=specs,
        out_specs=(pl.BlockSpec(memory_space=vmem), pl.BlockSpec(memory_space=vmem)),
        compiler_params=pltpu.CompilerParams(vmem_limit_bytes=48 * 1024 * 1024),
    )(*args)


REACH = 3
DOC_BLOCKS = 10
WIN_BLOCKS = 16


def shifted(shard, axis, by):
    length = lax.axis_size(axis)
    pairs = [(i, i + by) for i in range(length) if 0 <= i + by < length]
    return lax.ppermute(shard, axis, pairs)


def doc_index(positions, doc_bounds):
    flat = positions.reshape(-1)
    edges = doc_bounds[1:]
    counts = jnp.sum((edges[None, :] <= flat[:, None]).astype(jnp.int32), axis=1)
    return counts.reshape(positions.shape)


def local(query, key, value, attn_out, grad_out, log_norm, doc_bounds, local_pairs, ship_table):
    position = lax.axis_index("ctx")
    tokens, features = query.shape
    kv_features = key.shape[1]
    heads = log_norm.shape[0]
    own_blocks = tokens // BLOCK
    offsets = jnp.arange(BLOCK, dtype=jnp.int32)
    delta = jnp.einsum(
        "thd,thd->ht",
        grad_out.reshape(tokens, heads, HEAD_DIM),
        attn_out.reshape(tokens, heads, HEAD_DIM),
        preferred_element_type=jnp.float32,
    )
    own_keyval = jnp.concatenate([key, value], axis=1)
    first_used = min(max(REACH * own_blocks - DOC_BLOCKS, 0), own_blocks) * BLOCK
    pieces = []
    for hop in range(REACH, 0, -1):
        if hop == REACH:
            tail = shifted(own_keyval[first_used:], "ctx", hop)
            pieces.append(jnp.zeros((first_used, 2 * kv_features), own_keyval.dtype))
            pieces.append(tail)
        else:
            pieces.append(shifted(own_keyval, "ctx", hop))
    keyval_window = jnp.concatenate(pieces + [own_keyval], axis=0)
    first_block = position * own_blocks
    query_pos = (first_block + jnp.arange(own_blocks, dtype=jnp.int32))[:, None] * BLOCK + offsets
    window_first = first_block - REACH * own_blocks
    key_pos = (window_first * BLOCK + jnp.arange(WIN_BLOCKS * BLOCK, dtype=jnp.int32))
    own_ship = ship_table[position]
    ship_keys = own_ship[:, 1:]
    ship_queries = jnp.where(ship_keys >= 0, own_ship[:, :1], -1)
    ship_pairs = jnp.stack([ship_queries, ship_keys], axis=2).reshape(-1, 2)
    pairs = jnp.concatenate([local_pairs, ship_pairs], axis=0)
    query_grads, keyval_grads = run_pairs(
        pairs, query, grad_out, log_norm, delta, query_pos,
        keyval_window, key_pos, doc_bounds,
    )
    segments = keyval_grads.reshape(REACH + 1, own_blocks * BLOCK, 2 * kv_features)
    own_grads = segments[REACH]
    for hop in range(1, REACH):
        own_grads = own_grads + shifted(segments[REACH - hop], "ctx", -hop)
    far_grads = shifted(segments[0][first_used:], "ctx", -REACH)
    own_grads = own_grads.at[first_used:].add(far_grads)
    grad_query = query_grads.reshape(tokens, features).astype(jnp.bfloat16)
    grad_key = own_grads[:, :kv_features].astype(jnp.bfloat16)
    grad_value = own_grads[:, kv_features:].astype(jnp.bfloat16)
    return (grad_query, grad_key, grad_value)


def solution(mesh):
    in_specs = (
        P("ctx", "head"),
        P("ctx", "head"),
        P("ctx", "head"),
        P("ctx", "head"),
        P("ctx", "head"),
        P("head", "ctx"),
        P(),
        P("ctx", None),
        P(),
    )
    out_specs = (P("ctx", "head"), P("ctx", "head"), P("ctx", "head"))
    return jax.shard_map(local, mesh=mesh, in_specs=in_specs, out_specs=out_specs, check_vma=False)
```

```python
import functools
import jax
import jax.numpy as jnp
from jax import lax
from jax.experimental import pallas as pl
from jax.experimental.pallas import tpu as pltpu
from jax.sharding import PartitionSpec as P

HEAD_DIM = 128
BLOCK = 128

NT = (((1,), (1,)), ((), ()))
TN = (((0,), (0,)), ((), ()))


def pair_kernel(pairs_ref, q_ref, do_ref, norm_ref, delta_ref, qdoc_ref, qpos_ref,
                kdoc_ref, kpos_ref, kv_ref, dq_ref, dkv_ref):
    dq_ref[...] = jnp.zeros(dq_ref.shape, jnp.float32)
    dkv_ref[...] = jnp.zeros(dkv_ref.shape, jnp.float32)
    heads = norm_ref.shape[1] // BLOCK
    kv_features = kv_ref.shape[1] // 2
    kv_heads = kv_features // HEAD_DIM
    group = heads // kv_heads
    scale = HEAD_DIM ** (-0.5)

    def body(i, carry):
        qb_raw = pairs_ref[2 * i]
        kb_raw = pairs_ref[2 * i + 1]
        pl.when((qb_raw >= 0) & (kb_raw >= 0))(lambda: one_pair(jnp.maximum(qb_raw, 0), jnp.maximum(kb_raw, 0)))
        return carry

    def one_pair(qb, kb):
        qrow = pl.multiple_of(qb * BLOCK, BLOCK)
        krow = pl.multiple_of(kb * BLOCK, BLOCK)
        qdoc = qdoc_ref[pl.ds(qb, 1), :]
        qpos = qpos_ref[pl.ds(qb, 1), :]
        kdoc = kdoc_ref[pl.ds(krow, BLOCK), :]
        kpos = kpos_ref[pl.ds(krow, BLOCK), :]
        allowed = (kdoc == qdoc) & (kpos <= qpos)
        wide_allowed = jnp.concatenate([allowed] * group, axis=1)
        for g in range(kv_heads):
            k = kv_ref[pl.ds(krow, BLOCK), pl.ds(g * HEAD_DIM, HEAD_DIM)]
            v = kv_ref[pl.ds(krow, BLOCK), pl.ds(kv_features + g * HEAD_DIM, HEAD_DIM)]
            head_cols = [pl.ds((g * group + j) * HEAD_DIM, HEAD_DIM) for j in range(group)]
            q = jnp.concatenate([q_ref[pl.ds(qrow, BLOCK), c] for c in head_cols], axis=0)
            do = jnp.concatenate([do_ref[pl.ds(qrow, BLOCK), c] for c in head_cols], axis=0)
            group_cols = pl.ds(g * group * BLOCK, group * BLOCK)
            norm = norm_ref[pl.ds(qb, 1), group_cols]
            dl = delta_ref[pl.ds(qb, 1), group_cols]
            scores = lax.dot_general(k, q, NT, preferred_element_type=jnp.float32) * scale
            weights = jnp.where(wide_allowed, jnp.exp(scores - norm), 0.0)
            weight_grads = lax.dot_general(v, do, NT, preferred_element_type=jnp.float32)
            score_grads = (weights * (weight_grads - dl)).astype(jnp.bfloat16)
            weights_low = weights.astype(jnp.bfloat16)
            dv = jnp.dot(weights_low, do, preferred_element_type=jnp.float32)
            dk = jnp.dot(score_grads, q, preferred_element_type=jnp.float32)
            part_query = lax.dot_general(score_grads, k, TN, preferred_element_type=jnp.float32)
            for j, c in enumerate(head_cols):
                dq_ref[pl.ds(qrow, BLOCK), c] += part_query[j * BLOCK:(j + 1) * BLOCK]
            dkv_ref[pl.ds(krow, BLOCK), pl.ds(g * HEAD_DIM, HEAD_DIM)] += dk * scale
            dkv_ref[pl.ds(krow, BLOCK), pl.ds(kv_features + g * HEAD_DIM, HEAD_DIM)] += dv

    lax.fori_loop(0, pairs_ref.shape[0] // 2, body, 0)


def run_pairs(pairs, queries, outgrads, norms, deltas, query_pos, keyval, key_pos, doc_bounds):
    q_doc = doc_index(query_pos, doc_bounds)
    k_doc = doc_index(key_pos, doc_bounds)
    tokens, features = queries.shape
    window, both = keyval.shape
    heads = norms.shape[0]
    blocks = tokens // BLOCK
    norms = norms.reshape(heads, blocks, BLOCK).transpose(1, 0, 2).reshape(blocks, heads * BLOCK)
    deltas = deltas.reshape(heads, blocks, BLOCK).transpose(1, 0, 2).reshape(blocks, heads * BLOCK)
    vmem = pltpu.MemorySpace.VMEM
    smem = pltpu.MemorySpace.SMEM
    args = (
        pairs.reshape(-1).astype(jnp.int32),
        queries, outgrads, norms, deltas,
        q_doc, query_pos,
        k_doc.reshape(window, 1), key_pos.reshape(window, 1),
        keyval,
    )
    specs = [pl.BlockSpec(memory_space=smem)] + [pl.BlockSpec(memory_space=vmem)] * 9
    return pl.pallas_call(
        pair_kernel,
        out_shape=(
            jax.ShapeDtypeStruct((tokens, features), jnp.float32),
            jax.ShapeDtypeStruct((window, both), jnp.float32),
        ),
        in_specs=specs,
        out_specs=(pl.BlockSpec(memory_space=vmem), pl.BlockSpec(memory_space=vmem)),
        compiler_params=pltpu.CompilerParams(vmem_limit_bytes=48 * 1024 * 1024),
    )(*args)


REACH = 3
DOC_BLOCKS = 10
WIN_BLOCKS = 16


def shifted(shard, axis, by):
    length = lax.axis_size(axis)
    pairs = [(i, i + by) for i in range(length) if 0 <= i + by < length]
    return lax.ppermute(shard, axis, pairs)


def doc_index(positions, doc_bounds):
    flat = positions.reshape(-1)
    edges = doc_bounds[1:]
    counts = jnp.sum((edges[None, :] <= flat[:, None]).astype(jnp.int32), axis=1)
    return counts.reshape(positions.shape)


def local(query, key, value, attn_out, grad_out, log_norm, doc_bounds, local_pairs, ship_table):
    position = lax.axis_index("ctx")
    tokens, features = query.shape
    kv_features = key.shape[1]
    heads = log_norm.shape[0]
    own_blocks = tokens // BLOCK
    offsets = jnp.arange(BLOCK, dtype=jnp.int32)
    delta = jnp.einsum(
        "thd,thd->ht",
        grad_out.reshape(tokens, heads, HEAD_DIM),
        attn_out.reshape(tokens, heads, HEAD_DIM),
        preferred_element_type=jnp.float32,
    )
    own_keyval = jnp.concatenate([key, value], axis=1)
    first_used = min(max(REACH * own_blocks - DOC_BLOCKS, 0), own_blocks) * BLOCK
    pieces = []
    for hop in range(REACH, 0, -1):
        if hop == REACH:
            tail = shifted(own_keyval[first_used:], "ctx", hop)
            pieces.append(jnp.zeros((first_used, 2 * kv_features), own_keyval.dtype))
            pieces.append(tail)
        else:
            pieces.append(shifted(own_keyval, "ctx", hop))
    keyval_window = jnp.concatenate(pieces + [own_keyval], axis=0)
    first_block = position * own_blocks
    query_pos = (first_block + jnp.arange(own_blocks, dtype=jnp.int32))[:, None] * BLOCK + offsets
    window_first = first_block - REACH * own_blocks
    key_pos = (window_first * BLOCK + jnp.arange(WIN_BLOCKS * BLOCK, dtype=jnp.int32))
    own_ship = ship_table[position]
    ship_keys = own_ship[:, 1:]
    ship_queries = jnp.where(ship_keys >= 0, own_ship[:, :1], -1)
    ship_pairs = jnp.stack([ship_queries, ship_keys], axis=2).reshape(-1, 2)
    pairs = jnp.concatenate([local_pairs, ship_pairs], axis=0)
    query_grads, keyval_grads = run_pairs(
        pairs, query, grad_out, log_norm, delta, query_pos,
        keyval_window, key_pos, doc_bounds,
    )
    segments = keyval_grads.reshape(REACH + 1, own_blocks * BLOCK, 2 * kv_features)
    own_grads = segments[REACH]
    for hop in range(1, REACH):
        own_grads = own_grads + shifted(segments[REACH - hop].astype(jnp.bfloat16), "ctx", -hop)
    far_grads = shifted(segments[0][first_used:].astype(jnp.bfloat16), "ctx", -REACH)
    own_grads = own_grads.at[first_used:].add(far_grads.astype(jnp.float32))
    grad_query = (query_grads * HEAD_DIM ** (-0.5)).astype(jnp.bfloat16)
    grad_key = own_grads[:, :kv_features].astype(jnp.bfloat16)
    grad_value = own_grads[:, kv_features:].astype(jnp.bfloat16)
    return (grad_query, grad_key, grad_value)


def solution(mesh):
    in_specs = (
        P("ctx", "head"),
        P("ctx", "head"),
        P("ctx", "head"),
        P("ctx", "head"),
        P("ctx", "head"),
        P("head", "ctx"),
        P(),
        P("ctx", None),
        P(),
    )
    out_specs = (P("ctx", "head"), P("ctx", "head"), P("ctx", "head"))
    return jax.shard_map(local, mesh=mesh, in_specs=in_specs, out_specs=out_specs, check_vma=False)
```

```python
import functools
import jax
import jax.numpy as jnp
from jax import lax
from jax.experimental import pallas as pl
from jax.experimental.pallas import tpu as pltpu
from jax.sharding import PartitionSpec as P

HEAD_DIM = 128
BLOCK = 128

NT = (((1,), (1,)), ((), ()))
TN = (((0,), (0,)), ((), ()))


def pair_kernel(piece_starts, pairs_ref, q_ref, do_ref, norm_ref, delta_ref, qdoc_ref, qpos_ref,
                kdoc_ref, kpos_ref, *refs):
    piece_refs = refs[:len(piece_starts)]
    dq_ref, dkv_ref = refs[len(piece_starts):]
    dq_ref[...] = jnp.zeros(dq_ref.shape, jnp.float32)
    dkv_ref[...] = jnp.zeros(dkv_ref.shape, jnp.float32)
    heads = norm_ref.shape[1] // BLOCK
    kv_features = piece_refs[0].shape[1] // 2
    kv_heads = kv_features // HEAD_DIM
    group = heads // kv_heads
    scale = HEAD_DIM ** (-0.5)

    def body(i, carry):
        qb_raw = pairs_ref[2 * i]
        kb_raw = pairs_ref[2 * i + 1]
        live = (qb_raw >= 0) & (kb_raw >= 0)
        qb = jnp.maximum(qb_raw, 0)
        kb = jnp.maximum(kb_raw, 0)
        for start, kv_ref in zip(piece_starts, piece_refs):
            end = start + kv_ref.shape[0] // BLOCK
            inside = live & (kb >= start) & (kb < end)
            pl.when(inside)(functools.partial(one_pair, qb, kb, kv_ref, start))
        return carry

    def one_pair(qb, kb, kv_ref, start):
        local_row = pl.multiple_of((kb - start) * BLOCK, BLOCK)
        qrow = pl.multiple_of(qb * BLOCK, BLOCK)
        krow = pl.multiple_of(kb * BLOCK, BLOCK)
        qdoc = qdoc_ref[pl.ds(qb, 1), :]
        qpos = qpos_ref[pl.ds(qb, 1), :]
        kdoc = kdoc_ref[pl.ds(krow, BLOCK), :]
        kpos = kpos_ref[pl.ds(krow, BLOCK), :]
        allowed = (kdoc == qdoc) & (kpos <= qpos)
        wide_allowed = jnp.concatenate([allowed] * group, axis=1)
        for g in range(kv_heads):
            k = kv_ref[pl.ds(local_row, BLOCK), pl.ds(g * HEAD_DIM, HEAD_DIM)]
            v = kv_ref[pl.ds(local_row, BLOCK), pl.ds(kv_features + g * HEAD_DIM, HEAD_DIM)]
            head_cols = [pl.ds((g * group + j) * HEAD_DIM, HEAD_DIM) for j in range(group)]
            q = jnp.concatenate([q_ref[pl.ds(qrow, BLOCK), c] for c in head_cols], axis=0)
            do = jnp.concatenate([do_ref[pl.ds(qrow, BLOCK), c] for c in head_cols], axis=0)
            group_cols = pl.ds(g * group * BLOCK, group * BLOCK)
            norm = norm_ref[pl.ds(qb, 1), group_cols]
            dl = delta_ref[pl.ds(qb, 1), group_cols]
            scores = lax.dot_general(k, q, NT, preferred_element_type=jnp.float32) * scale
            weights = jnp.where(wide_allowed, jnp.exp(scores - norm), 0.0)
            weight_grads = lax.dot_general(v, do, NT, preferred_element_type=jnp.float32)
            score_grads = (weights * (weight_grads - dl)).astype(jnp.bfloat16)
            weights_low = weights.astype(jnp.bfloat16)
            dv = jnp.dot(weights_low, do, preferred_element_type=jnp.float32)
            dk = jnp.dot(score_grads, q, preferred_element_type=jnp.float32)
            part_query = lax.dot_general(score_grads, k, TN, preferred_element_type=jnp.float32)
            for j, c in enumerate(head_cols):
                dq_ref[pl.ds(qrow, BLOCK), c] += part_query[j * BLOCK:(j + 1) * BLOCK]
            dkv_ref[pl.ds(krow, BLOCK), pl.ds(g * HEAD_DIM, HEAD_DIM)] += dk * scale
            dkv_ref[pl.ds(krow, BLOCK), pl.ds(kv_features + g * HEAD_DIM, HEAD_DIM)] += dv

    lax.fori_loop(0, pairs_ref.shape[0] // 2, body, 0)


def run_pairs(pairs, queries, outgrads, norms, deltas, query_pos, pieces, key_pos, doc_bounds):
    q_doc = doc_index(query_pos, doc_bounds)
    k_doc = doc_index(key_pos, doc_bounds)
    tokens, features = queries.shape
    window = key_pos.shape[0]
    both = pieces[0][1].shape[1]
    heads = norms.shape[0]
    blocks = tokens // BLOCK
    norms = norms.reshape(heads, blocks, BLOCK).transpose(1, 0, 2).reshape(blocks, heads * BLOCK)
    vmem = pltpu.MemorySpace.VMEM
    smem = pltpu.MemorySpace.SMEM
    args = (
        pairs.reshape(-1).astype(jnp.int32),
        queries, outgrads, norms, deltas,
        q_doc, query_pos,
        k_doc.reshape(window, 1), key_pos.reshape(window, 1),
    ) + tuple(rows for _, rows in pieces)
    specs = [pl.BlockSpec(memory_space=smem)] + [pl.BlockSpec(memory_space=vmem)] * (len(args) - 1)
    kernel = functools.partial(pair_kernel, tuple(start for start, _ in pieces))
    return pl.pallas_call(
        kernel,
        out_shape=(
            jax.ShapeDtypeStruct((tokens, features), jnp.float32),
            jax.ShapeDtypeStruct((window, both), jnp.float32),
        ),
        in_specs=specs,
        out_specs=(pl.BlockSpec(memory_space=vmem), pl.BlockSpec(memory_space=vmem)),
        compiler_params=pltpu.CompilerParams(vmem_limit_bytes=48 * 1024 * 1024),
    )(*args)


REACH = 3
DOC_BLOCKS = 10
WIN_BLOCKS = 16


def shifted(shard, axis, by):
    length = lax.axis_size(axis)
    pairs = [(i, i + by) for i in range(length) if 0 <= i + by < length]
    return lax.ppermute(shard, axis, pairs)


def doc_index(positions, doc_bounds):
    flat = positions.reshape(-1)
    edges = doc_bounds[1:]
    counts = jnp.sum((edges[None, :] <= flat[:, None]).astype(jnp.int32), axis=1)
    return counts.reshape(positions.shape)


def local(query, key, value, attn_out, grad_out, log_norm, doc_bounds, local_pairs, ship_table):
    position = lax.axis_index("ctx")
    tokens, features = query.shape
    kv_features = key.shape[1]
    heads = log_norm.shape[0]
    own_blocks = tokens // BLOCK
    offsets = jnp.arange(BLOCK, dtype=jnp.int32)
    products = grad_out.astype(jnp.float32) * attn_out.astype(jnp.float32)
    delta = jnp.sum(products.reshape(tokens, heads, HEAD_DIM), axis=2)
    delta = delta.reshape(own_blocks, BLOCK, heads).transpose(0, 2, 1).reshape(own_blocks, heads * BLOCK)
    own_keyval = jnp.concatenate([key, value], axis=1)
    first_used = min(max(REACH * own_blocks - DOC_BLOCKS, 0), own_blocks) * BLOCK
    pieces = [(first_used // BLOCK, shifted(own_keyval[first_used:], "ctx", REACH))]
    for hop in range(REACH - 1, 0, -1):
        pieces.append(((REACH - hop) * own_blocks, shifted(own_keyval, "ctx", hop)))
    pieces.append((REACH * own_blocks, own_keyval))
    first_block = position * own_blocks
    query_pos = (first_block + jnp.arange(own_blocks, dtype=jnp.int32))[:, None] * BLOCK + offsets
    window_first = first_block - REACH * own_blocks
    key_pos = (window_first * BLOCK + jnp.arange(WIN_BLOCKS * BLOCK, dtype=jnp.int32))
    own_ship = ship_table[position]
    ship_keys = own_ship[:, 1:]
    ship_queries = jnp.where(ship_keys >= 0, own_ship[:, :1], -1)
    ship_pairs = jnp.stack([ship_queries, ship_keys], axis=2).reshape(-1, 2)
    pairs = jnp.concatenate([local_pairs, ship_pairs], axis=0)
    query_grads, keyval_grads = run_pairs(
        pairs, query, grad_out, log_norm, delta, query_pos,
        pieces, key_pos, doc_bounds,
    )
    segments = keyval_grads.reshape(REACH + 1, own_blocks * BLOCK, 2 * kv_features)
    own_grads = segments[REACH]
    for hop in range(1, REACH):
        own_grads = own_grads + shifted(segments[REACH - hop].astype(jnp.bfloat16), "ctx", -hop)
    far_grads = shifted(segments[0][first_used:].astype(jnp.bfloat16), "ctx", -REACH)
    own_grads = own_grads.at[first_used:].add(far_grads.astype(jnp.float32))
    grad_query = (query_grads * HEAD_DIM ** (-0.5)).astype(jnp.bfloat16)
    grad_key = own_grads[:, :kv_features].astype(jnp.bfloat16)
    grad_value = own_grads[:, kv_features:].astype(jnp.bfloat16)
    return (grad_query, grad_key, grad_value)


def solution(mesh):
    in_specs = (
        P("ctx", "head"),
        P("ctx", "head"),
        P("ctx", "head"),
        P("ctx", "head"),
        P("ctx", "head"),
        P("head", "ctx"),
        P(),
        P("ctx", None),
        P(),
    )
    out_specs = (P("ctx", "head"), P("ctx", "head"), P("ctx", "head"))
    return jax.shard_map(local, mesh=mesh, in_specs=in_specs, out_specs=out_specs, check_vma=False)
```

```python
import functools
import jax
import jax.numpy as jnp
from jax import lax
from jax.experimental import pallas as pl
from jax.experimental.pallas import tpu as pltpu
from jax.sharding import PartitionSpec as P

HEAD_DIM = 128
BLOCK = 128

NT = (((1,), (1,)), ((), ()))
TN = (((0,), (0,)), ((), ()))


def pair_kernel(piece_starts, pairs_ref, q_ref, do_ref, o_ref, norm_ref, qdoc_ref, qpos_ref,
                kdoc_ref, kpos_ref, *refs):
    piece_refs = refs[:len(piece_starts)]
    dq_ref, dkv_ref, delta_ref = refs[len(piece_starts):]
    dq_ref[...] = jnp.zeros(dq_ref.shape, jnp.float32)
    dkv_ref[...] = jnp.zeros(dkv_ref.shape, jnp.float32)
    heads = norm_ref.shape[1] // BLOCK
    kv_features = piece_refs[0].shape[1] // 2
    kv_heads = kv_features // HEAD_DIM
    group = heads // kv_heads
    scale = HEAD_DIM ** (-0.5)

    def one_delta(qb, carry):
        rows = pl.ds(pl.multiple_of(qb * BLOCK, BLOCK), BLOCK)
        for h in range(heads):
            cols = pl.ds(h * HEAD_DIM, HEAD_DIM)
            prod = do_ref[rows, cols].astype(jnp.float32) * o_ref[rows, cols].astype(jnp.float32)
            delta_ref[qb, :, pl.ds(h * BLOCK, BLOCK)] = jnp.sum(prod.T, axis=0, keepdims=True)
        return carry

    lax.fori_loop(0, q_ref.shape[0] // BLOCK, one_delta, 0)

    def body(i, carry):
        qb_raw = pairs_ref[2 * i]
        kb_raw = pairs_ref[2 * i + 1]
        live = (qb_raw >= 0) & (kb_raw >= 0)
        qb = jnp.maximum(qb_raw, 0)
        kb = jnp.maximum(kb_raw, 0)
        for start, kv_ref in zip(piece_starts, piece_refs):
            end = start + kv_ref.shape[0] // BLOCK
            inside = live & (kb >= start) & (kb < end)
            pl.when(inside)(functools.partial(one_pair, qb, kb, kv_ref, start))
        return carry

    def one_pair(qb, kb, kv_ref, start):
        local_row = pl.multiple_of((kb - start) * BLOCK, BLOCK)
        qrow = pl.multiple_of(qb * BLOCK, BLOCK)
        krow = pl.multiple_of(kb * BLOCK, BLOCK)
        qdoc = qdoc_ref[pl.ds(qb, 1), :]
        qpos = qpos_ref[pl.ds(qb, 1), :]
        kdoc = kdoc_ref[pl.ds(krow, BLOCK), :]
        kpos = kpos_ref[pl.ds(krow, BLOCK), :]
        allowed = (kdoc == qdoc) & (kpos <= qpos)
        wide_allowed = jnp.concatenate([allowed] * group, axis=1)
        for g in range(kv_heads):
            k = kv_ref[pl.ds(local_row, BLOCK), pl.ds(g * HEAD_DIM, HEAD_DIM)]
            v = kv_ref[pl.ds(local_row, BLOCK), pl.ds(kv_features + g * HEAD_DIM, HEAD_DIM)]
            head_cols = [pl.ds((g * group + j) * HEAD_DIM, HEAD_DIM) for j in range(group)]
            q = jnp.concatenate([q_ref[pl.ds(qrow, BLOCK), c] for c in head_cols], axis=0)
            do = jnp.concatenate([do_ref[pl.ds(qrow, BLOCK), c] for c in head_cols], axis=0)
            group_cols = pl.ds(g * group * BLOCK, group * BLOCK)
            norm = norm_ref[pl.ds(qb, 1), group_cols]
            dl = delta_ref[qb, :, group_cols]
            scores = lax.dot_general(k, q, NT, preferred_element_type=jnp.float32) * scale
            weights = jnp.where(wide_allowed, jnp.exp(scores - norm), 0.0)
            weight_grads = lax.dot_general(v, do, NT, preferred_element_type=jnp.float32)
            score_grads = (weights * (weight_grads - dl)).astype(jnp.bfloat16)
            weights_low = weights.astype(jnp.bfloat16)
            dv = jnp.dot(weights_low, do, preferred_element_type=jnp.float32)
            dk = jnp.dot(score_grads, q, preferred_element_type=jnp.float32)
            part_query = lax.dot_general(score_grads, k, TN, preferred_element_type=jnp.float32)
            for j, c in enumerate(head_cols):
                dq_ref[pl.ds(qrow, BLOCK), c] += part_query[j * BLOCK:(j + 1) * BLOCK]
            dkv_ref[pl.ds(krow, BLOCK), pl.ds(g * HEAD_DIM, HEAD_DIM)] += dk * scale
            dkv_ref[pl.ds(krow, BLOCK), pl.ds(kv_features + g * HEAD_DIM, HEAD_DIM)] += dv

    lax.fori_loop(0, pairs_ref.shape[0] // 2, body, 0)


def run_pairs(pairs, queries, outgrads, outputs, norms, query_pos, pieces, key_pos, doc_bounds):
    q_doc = doc_index(query_pos, doc_bounds)
    k_doc = doc_index(key_pos, doc_bounds)
    tokens, features = queries.shape
    window = key_pos.shape[0]
    both = pieces[0][1].shape[1]
    heads = norms.shape[0]
    blocks = tokens // BLOCK
    norms = norms.reshape(heads, blocks, BLOCK).transpose(1, 0, 2).reshape(blocks, heads * BLOCK)
    vmem = pltpu.MemorySpace.VMEM
    smem = pltpu.MemorySpace.SMEM
    args = (
        pairs.reshape(-1).astype(jnp.int32),
        queries, outgrads, outputs, norms,
        q_doc, query_pos,
        k_doc.reshape(window, 1), key_pos.reshape(window, 1),
    ) + tuple(rows for _, rows in pieces)
    specs = [pl.BlockSpec(memory_space=smem)] + [pl.BlockSpec(memory_space=vmem)] * (len(args) - 1)
    kernel = functools.partial(pair_kernel, tuple(start for start, _ in pieces))
    return pl.pallas_call(
        kernel,
        out_shape=(
            jax.ShapeDtypeStruct((tokens, features), jnp.float32),
            jax.ShapeDtypeStruct((window, both), jnp.float32),
        ),
        in_specs=specs,
        out_specs=(pl.BlockSpec(memory_space=vmem), pl.BlockSpec(memory_space=vmem)),
        scratch_shapes=[pltpu.VMEM((blocks, 1, heads * BLOCK), jnp.float32)],
        compiler_params=pltpu.CompilerParams(vmem_limit_bytes=48 * 1024 * 1024),
    )(*args)


REACH = 3
DOC_BLOCKS = 10
WIN_BLOCKS = 16


def shifted(shard, axis, by):
    length = lax.axis_size(axis)
    pairs = [(i, i + by) for i in range(length) if 0 <= i + by < length]
    return lax.ppermute(shard, axis, pairs)


def doc_index(positions, doc_bounds):
    flat = positions.reshape(-1)
    edges = doc_bounds[1:]
    counts = jnp.sum((edges[None, :] <= flat[:, None]).astype(jnp.int32), axis=1)
    return counts.reshape(positions.shape)


def local(query, key, value, attn_out, grad_out, log_norm, doc_bounds, local_pairs, ship_table):
    position = lax.axis_index("ctx")
    tokens, features = query.shape
    kv_features = key.shape[1]
    heads = log_norm.shape[0]
    own_blocks = tokens // BLOCK
    offsets = jnp.arange(BLOCK, dtype=jnp.int32)
    own_keyval = jnp.concatenate([key, value], axis=1)
    first_used = min(max(REACH * own_blocks - DOC_BLOCKS, 0), own_blocks) * BLOCK
    pieces = [(first_used // BLOCK, shifted(own_keyval[first_used:], "ctx", REACH))]
    for hop in range(REACH - 1, 0, -1):
        pieces.append(((REACH - hop) * own_blocks, shifted(own_keyval, "ctx", hop)))
    pieces.append((REACH * own_blocks, own_keyval))
    first_block = position * own_blocks
    query_pos = (first_block + jnp.arange(own_blocks, dtype=jnp.int32))[:, None] * BLOCK + offsets
    window_first = first_block - REACH * own_blocks
    key_pos = (window_first * BLOCK + jnp.arange(WIN_BLOCKS * BLOCK, dtype=jnp.int32))
    own_ship = ship_table[position]
    ship_keys = own_ship[:, 1:]
    ship_queries = jnp.where(ship_keys >= 0, own_ship[:, :1], -1)
    ship_pairs = jnp.stack([ship_queries, ship_keys], axis=2).reshape(-1, 2)
    pairs = jnp.concatenate([local_pairs, ship_pairs], axis=0)
    query_grads, keyval_grads = run_pairs(
        pairs, query, grad_out, attn_out, log_norm, query_pos,
        pieces, key_pos, doc_bounds,
    )
    segments = keyval_grads.reshape(REACH + 1, own_blocks * BLOCK, 2 * kv_features)
    own_grads = segments[REACH]
    for hop in range(1, REACH):
        own_grads = own_grads + shifted(segments[REACH - hop].astype(jnp.bfloat16), "ctx", -hop)
    far_grads = shifted(segments[0][first_used:].astype(jnp.bfloat16), "ctx", -REACH)
    own_grads = own_grads.at[first_used:].add(far_grads.astype(jnp.float32))
    grad_query = (query_grads * HEAD_DIM ** (-0.5)).astype(jnp.bfloat16)
    grad_key = own_grads[:, :kv_features].astype(jnp.bfloat16)
    grad_value = own_grads[:, kv_features:].astype(jnp.bfloat16)
    return (grad_query, grad_key, grad_value)


def solution(mesh):
    in_specs = (
        P("ctx", "head"),
        P("ctx", "head"),
        P("ctx", "head"),
        P("ctx", "head"),
        P("ctx", "head"),
        P("head", "ctx"),
        P(),
        P("ctx", None),
        P(),
    )
    out_specs = (P("ctx", "head"), P("ctx", "head"), P("ctx", "head"))
    return jax.shard_map(local, mesh=mesh, in_specs=in_specs, out_specs=out_specs, check_vma=False)
```

```python
import functools
import jax
import jax.numpy as jnp
from jax import lax
from jax.experimental import pallas as pl
from jax.experimental.pallas import tpu as pltpu
from jax.sharding import PartitionSpec as P

HEAD_DIM = 128
BLOCK = 128

NT = (((1,), (1,)), ((), ()))
TN = (((0,), (0,)), ((), ()))


def pair_kernel(piece_starts, pairs_ref, whole_ref, q_ref, do_ref, o_ref, norm_ref, qdoc_ref, qpos_ref,
                kdoc_ref, kpos_ref, *refs):
    piece_refs = refs[:len(piece_starts)]
    dq_ref, dkv_ref, delta_ref = refs[len(piece_starts):]
    dq_ref[...] = jnp.zeros(dq_ref.shape, jnp.float32)
    dkv_ref[...] = jnp.zeros(dkv_ref.shape, jnp.float32)
    heads = norm_ref.shape[1] // BLOCK
    kv_features = piece_refs[0].shape[1] // 2
    kv_heads = kv_features // HEAD_DIM
    group = heads // kv_heads
    scale = HEAD_DIM ** (-0.5)

    def one_delta(qb, carry):
        rows = pl.ds(pl.multiple_of(qb * BLOCK, BLOCK), BLOCK)
        for h in range(heads):
            cols = pl.ds(h * HEAD_DIM, HEAD_DIM)
            prod = do_ref[rows, cols].astype(jnp.float32) * o_ref[rows, cols].astype(jnp.float32)
            delta_ref[qb, :, pl.ds(h * BLOCK, BLOCK)] = jnp.sum(prod.T, axis=0, keepdims=True)
        return carry

    lax.fori_loop(0, q_ref.shape[0] // BLOCK, one_delta, 0)

    def body(i, carry):
        qb_raw = pairs_ref[2 * i]
        kb_raw = pairs_ref[2 * i + 1]
        live = (qb_raw >= 0) & (kb_raw >= 0)
        qb = jnp.maximum(qb_raw, 0)
        kb = jnp.maximum(kb_raw, 0)
        whole = whole_ref[i] > 0
        for start, kv_ref in zip(piece_starts, piece_refs):
            end = start + kv_ref.shape[0] // BLOCK
            inside = live & (kb >= start) & (kb < end)
            pl.when(inside & whole)(functools.partial(one_pair, qb, kb, kv_ref, start, False))
            pl.when(inside & jnp.logical_not(whole))(
                functools.partial(one_pair, qb, kb, kv_ref, start, True))
        return carry

    def one_pair(qb, kb, kv_ref, start, masked):
        local_row = pl.multiple_of((kb - start) * BLOCK, BLOCK)
        qrow = pl.multiple_of(qb * BLOCK, BLOCK)
        krow = pl.multiple_of(kb * BLOCK, BLOCK)
        if masked:
            qdoc = qdoc_ref[pl.ds(qb, 1), :]
            qpos = qpos_ref[pl.ds(qb, 1), :]
            kdoc = kdoc_ref[pl.ds(krow, BLOCK), :]
            kpos = kpos_ref[pl.ds(krow, BLOCK), :]
            allowed = (kdoc == qdoc) & (kpos <= qpos)
            wide_allowed = jnp.concatenate([allowed] * group, axis=1)
        for g in range(kv_heads):
            k = kv_ref[pl.ds(local_row, BLOCK), pl.ds(g * HEAD_DIM, HEAD_DIM)]
            v = kv_ref[pl.ds(local_row, BLOCK), pl.ds(kv_features + g * HEAD_DIM, HEAD_DIM)]
            head_cols = [pl.ds((g * group + j) * HEAD_DIM, HEAD_DIM) for j in range(group)]
            q = jnp.concatenate([q_ref[pl.ds(qrow, BLOCK), c] for c in head_cols], axis=0)
            do = jnp.concatenate([do_ref[pl.ds(qrow, BLOCK), c] for c in head_cols], axis=0)
            group_cols = pl.ds(g * group * BLOCK, group * BLOCK)
            norm = norm_ref[pl.ds(qb, 1), group_cols]
            dl = delta_ref[qb, :, group_cols]
            scores = lax.dot_general(k, q, NT, preferred_element_type=jnp.float32) * scale
            weights = jnp.exp(scores - norm)
            if masked:
                weights = jnp.where(wide_allowed, weights, 0.0)
            weight_grads = lax.dot_general(v, do, NT, preferred_element_type=jnp.float32)
            score_grads = (weights * (weight_grads - dl)).astype(jnp.bfloat16)
            weights_low = weights.astype(jnp.bfloat16)
            dv = jnp.dot(weights_low, do, preferred_element_type=jnp.float32)
            dk = jnp.dot(score_grads, q, preferred_element_type=jnp.float32)
            part_query = lax.dot_general(score_grads, k, TN, preferred_element_type=jnp.float32)
            for j, c in enumerate(head_cols):
                dq_ref[pl.ds(qrow, BLOCK), c] += part_query[j * BLOCK:(j + 1) * BLOCK]
            dkv_ref[pl.ds(krow, BLOCK), pl.ds(g * HEAD_DIM, HEAD_DIM)] += dk * scale
            dkv_ref[pl.ds(krow, BLOCK), pl.ds(kv_features + g * HEAD_DIM, HEAD_DIM)] += dv

    lax.fori_loop(0, pairs_ref.shape[0] // 2, body, 0)


def run_pairs(pairs, queries, outgrads, outputs, norms, query_pos, pieces, key_pos, doc_bounds):
    q_doc = doc_index(query_pos, doc_bounds)
    k_doc = doc_index(key_pos, doc_bounds)
    tokens, features = queries.shape
    window = key_pos.shape[0]
    both = pieces[0][1].shape[1]
    heads = norms.shape[0]
    blocks = tokens // BLOCK
    norms = norms.reshape(heads, blocks, BLOCK).transpose(1, 0, 2).reshape(blocks, heads * BLOCK)
    vmem = pltpu.MemorySpace.VMEM
    smem = pltpu.MemorySpace.SMEM
    query_block = jnp.maximum(pairs[:, 0], 0)
    key_first = jnp.maximum(pairs[:, 1], 0) * BLOCK
    whole = (k_doc[key_first] == q_doc[query_block, BLOCK - 1]) & (
        key_pos[key_first + BLOCK - 1] <= query_pos[query_block, 0]
    )
    args = (
        pairs.reshape(-1).astype(jnp.int32),
        whole.astype(jnp.int32),
        queries, outgrads, outputs, norms,
        q_doc, query_pos,
        k_doc.reshape(window, 1), key_pos.reshape(window, 1),
    ) + tuple(rows for _, rows in pieces)
    specs = [pl.BlockSpec(memory_space=smem)] * 2 + [pl.BlockSpec(memory_space=vmem)] * (len(args) - 2)
    kernel = functools.partial(pair_kernel, tuple(start for start, _ in pieces))
    return pl.pallas_call(
        kernel,
        out_shape=(
            jax.ShapeDtypeStruct((tokens, features), jnp.float32),
            jax.ShapeDtypeStruct((window, both), jnp.float32),
        ),
        in_specs=specs,
        out_specs=(pl.BlockSpec(memory_space=vmem), pl.BlockSpec(memory_space=vmem)),
        scratch_shapes=[pltpu.VMEM((blocks, 1, heads * BLOCK), jnp.float32)],
        compiler_params=pltpu.CompilerParams(vmem_limit_bytes=48 * 1024 * 1024),
    )(*args)


REACH = 3
DOC_BLOCKS = 10
WIN_BLOCKS = 16


def shifted(shard, axis, by):
    length = lax.axis_size(axis)
    pairs = [(i, i + by) for i in range(length) if 0 <= i + by < length]
    return lax.ppermute(shard, axis, pairs)


def doc_index(positions, doc_bounds):
    flat = positions.reshape(-1)
    edges = doc_bounds[1:]
    counts = jnp.sum((edges[None, :] <= flat[:, None]).astype(jnp.int32), axis=1)
    return counts.reshape(positions.shape)


def local(query, key, value, attn_out, grad_out, log_norm, doc_bounds, local_pairs, ship_table):
    position = lax.axis_index("ctx")
    tokens, features = query.shape
    kv_features = key.shape[1]
    heads = log_norm.shape[0]
    own_blocks = tokens // BLOCK
    offsets = jnp.arange(BLOCK, dtype=jnp.int32)
    own_keyval = jnp.concatenate([key, value], axis=1)
    first_used = min(max(REACH * own_blocks - DOC_BLOCKS, 0), own_blocks) * BLOCK
    pieces = [(first_used // BLOCK, shifted(own_keyval[first_used:], "ctx", REACH))]
    for hop in range(REACH - 1, 0, -1):
        pieces.append(((REACH - hop) * own_blocks, shifted(own_keyval, "ctx", hop)))
    pieces.append((REACH * own_blocks, own_keyval))
    first_block = position * own_blocks
    query_pos = (first_block + jnp.arange(own_blocks, dtype=jnp.int32))[:, None] * BLOCK + offsets
    window_first = first_block - REACH * own_blocks
    key_pos = (window_first * BLOCK + jnp.arange(WIN_BLOCKS * BLOCK, dtype=jnp.int32))
    own_ship = ship_table[position]
    ship_keys = own_ship[:, 1:]
    ship_queries = jnp.where(ship_keys >= 0, own_ship[:, :1], -1)
    ship_pairs = jnp.stack([ship_queries, ship_keys], axis=2).reshape(-1, 2)
    pairs = jnp.concatenate([local_pairs, ship_pairs], axis=0)
    query_grads, keyval_grads = run_pairs(
        pairs, query, grad_out, attn_out, log_norm, query_pos,
        pieces, key_pos, doc_bounds,
    )
    segments = keyval_grads.reshape(REACH + 1, own_blocks * BLOCK, 2 * kv_features)
    own_grads = segments[REACH]
    for hop in range(1, REACH):
        own_grads = own_grads + shifted(segments[REACH - hop].astype(jnp.bfloat16), "ctx", -hop)
    far_grads = shifted(segments[0][first_used:].astype(jnp.bfloat16), "ctx", -REACH)
    own_grads = own_grads.at[first_used:].add(far_grads.astype(jnp.float32))
    grad_query = (query_grads * HEAD_DIM ** (-0.5)).astype(jnp.bfloat16)
    grad_key = own_grads[:, :kv_features].astype(jnp.bfloat16)
    grad_value = own_grads[:, kv_features:].astype(jnp.bfloat16)
    return (grad_query, grad_key, grad_value)


def solution(mesh):
    in_specs = (
        P("ctx", "head"),
        P("ctx", "head"),
        P("ctx", "head"),
        P("ctx", "head"),
        P("ctx", "head"),
        P("head", "ctx"),
        P(),
        P("ctx", None),
        P(),
    )
    out_specs = (P("ctx", "head"), P("ctx", "head"), P("ctx", "head"))
    return jax.shard_map(local, mesh=mesh, in_specs=in_specs, out_specs=out_specs, check_vma=False)
```

```python
import functools
import jax
import jax.numpy as jnp
from jax import lax
from jax.experimental import pallas as pl
from jax.experimental.pallas import tpu as pltpu
from jax.sharding import PartitionSpec as P

HEAD_DIM = 128
BLOCK = 128

NT = (((1,), (1,)), ((), ()))
TN = (((0,), (0,)), ((), ()))


def pair_kernel(piece_starts, pairs_ref, q_ref, do_ref, o_ref, norm_ref, qdoc_ref, qpos_ref,
                kdoc_ref, kpos_ref, *refs):
    piece_refs = refs[:len(piece_starts)]
    dq_out, far_out, own_out, delta_ref, dq_ref, dkv_ref = refs[len(piece_starts):]
    dq_ref[...] = jnp.zeros(dq_ref.shape, jnp.float32)
    dkv_ref[...] = jnp.zeros(dkv_ref.shape, jnp.float32)
    heads = norm_ref.shape[1] // BLOCK
    kv_features = piece_refs[0].shape[1] // 2
    kv_heads = kv_features // HEAD_DIM
    group = heads // kv_heads
    scale = HEAD_DIM ** (-0.5)

    def one_delta(qb, carry):
        rows = pl.ds(pl.multiple_of(qb * BLOCK, BLOCK), BLOCK)
        for h in range(heads):
            cols = pl.ds(h * HEAD_DIM, HEAD_DIM)
            prod = do_ref[rows, cols].astype(jnp.float32) * o_ref[rows, cols].astype(jnp.float32)
            delta_ref[qb, :, pl.ds(h * BLOCK, BLOCK)] = jnp.sum(prod.T, axis=0, keepdims=True)
        return carry

    lax.fori_loop(0, q_ref.shape[0] // BLOCK, one_delta, 0)

    def body(i, carry):
        qb_raw = pairs_ref[2 * i]
        kb_raw = pairs_ref[2 * i + 1]
        live = (qb_raw >= 0) & (kb_raw >= 0)
        qb = jnp.maximum(qb_raw, 0)
        kb = jnp.maximum(kb_raw, 0)
        for start, kv_ref in zip(piece_starts, piece_refs):
            end = start + kv_ref.shape[0] // BLOCK
            inside = live & (kb >= start) & (kb < end)
            pl.when(inside)(functools.partial(one_pair, qb, kb, kv_ref, start))
        return carry

    def one_pair(qb, kb, kv_ref, start):
        local_row = pl.multiple_of((kb - start) * BLOCK, BLOCK)
        qrow = pl.multiple_of(qb * BLOCK, BLOCK)
        krow = pl.multiple_of(kb * BLOCK, BLOCK)
        qdoc = qdoc_ref[pl.ds(qb, 1), :]
        qpos = qpos_ref[pl.ds(qb, 1), :]
        kdoc = kdoc_ref[pl.ds(krow, BLOCK), :]
        kpos = kpos_ref[pl.ds(krow, BLOCK), :]
        allowed = (kdoc == qdoc) & (kpos <= qpos)
        wide_allowed = jnp.concatenate([allowed] * group, axis=1)
        for g in range(kv_heads):
            k = kv_ref[pl.ds(local_row, BLOCK), pl.ds(g * HEAD_DIM, HEAD_DIM)]
            v = kv_ref[pl.ds(local_row, BLOCK), pl.ds(kv_features + g * HEAD_DIM, HEAD_DIM)]
            head_cols = [pl.ds((g * group + j) * HEAD_DIM, HEAD_DIM) for j in range(group)]
            q = jnp.concatenate([q_ref[pl.ds(qrow, BLOCK), c] for c in head_cols], axis=0)
            do = jnp.concatenate([do_ref[pl.ds(qrow, BLOCK), c] for c in head_cols], axis=0)
            group_cols = pl.ds(g * group * BLOCK, group * BLOCK)
            norm = norm_ref[pl.ds(qb, 1), group_cols]
            dl = delta_ref[qb, :, group_cols]
            scores = lax.dot_general(k, q, NT, preferred_element_type=jnp.float32) * scale
            weights = jnp.where(wide_allowed, jnp.exp(scores - norm), 0.0)
            weight_grads = lax.dot_general(v, do, NT, preferred_element_type=jnp.float32)
            score_grads = (weights * (weight_grads - dl)).astype(jnp.bfloat16)
            weights_low = weights.astype(jnp.bfloat16)
            dv = jnp.dot(weights_low, do, preferred_element_type=jnp.float32)
            dk = jnp.dot(score_grads, q, preferred_element_type=jnp.float32)
            part_query = lax.dot_general(score_grads, k, TN, preferred_element_type=jnp.float32)
            for j, c in enumerate(head_cols):
                dq_ref[pl.ds(qrow, BLOCK), c] += part_query[j * BLOCK:(j + 1) * BLOCK]
            dkv_ref[pl.ds(krow, BLOCK), pl.ds(g * HEAD_DIM, HEAD_DIM)] += dk * scale
            dkv_ref[pl.ds(krow, BLOCK), pl.ds(kv_features + g * HEAD_DIM, HEAD_DIM)] += dv

    lax.fori_loop(0, pairs_ref.shape[0] // 2, body, 0)

    def finish_query(qb, carry):
        rows = pl.ds(pl.multiple_of(qb * BLOCK, BLOCK), BLOCK)
        dq_out[rows, :] = (dq_ref[rows, :] * scale).astype(dq_out.dtype)
        return carry

    lax.fori_loop(0, dq_ref.shape[0] // BLOCK, finish_query, 0)
    far_rows = far_out.shape[0]
    far_out[...] = dkv_ref[pl.ds(0, far_rows), :].astype(far_out.dtype)
    own_out[...] = dkv_ref[pl.ds(far_rows, own_out.shape[0]), :]


def run_pairs(pairs, queries, outgrads, outputs, norms, query_pos, pieces, key_pos, doc_bounds):
    q_doc = doc_index(query_pos, doc_bounds)
    k_doc = doc_index(key_pos, doc_bounds)
    tokens, features = queries.shape
    window = key_pos.shape[0]
    both = pieces[0][1].shape[1]
    own_rows = pieces[-1][1].shape[0]
    heads = norms.shape[0]
    blocks = tokens // BLOCK
    norms = norms.reshape(heads, blocks, BLOCK).transpose(1, 0, 2).reshape(blocks, heads * BLOCK)
    vmem = pltpu.MemorySpace.VMEM
    smem = pltpu.MemorySpace.SMEM
    args = (
        pairs.reshape(-1).astype(jnp.int32),
        queries, outgrads, outputs, norms,
        q_doc, query_pos,
        k_doc.reshape(window, 1), key_pos.reshape(window, 1),
    ) + tuple(rows for _, rows in pieces)
    specs = [pl.BlockSpec(memory_space=smem)] + [pl.BlockSpec(memory_space=vmem)] * (len(args) - 1)
    kernel = functools.partial(pair_kernel, tuple(start for start, _ in pieces))
    return pl.pallas_call(
        kernel,
        out_shape=(
            jax.ShapeDtypeStruct((tokens, features), jnp.bfloat16),
            jax.ShapeDtypeStruct((window - own_rows, both), jnp.bfloat16),
            jax.ShapeDtypeStruct((own_rows, both), jnp.float32),
        ),
        in_specs=specs,
        out_specs=tuple(pl.BlockSpec(memory_space=vmem) for _ in range(3)),
        scratch_shapes=[
            pltpu.VMEM((blocks, 1, heads * BLOCK), jnp.float32),
            pltpu.VMEM((tokens, features), jnp.float32),
            pltpu.VMEM((window, both), jnp.float32),
        ],
        compiler_params=pltpu.CompilerParams(vmem_limit_bytes=48 * 1024 * 1024),
    )(*args)


REACH = 3
DOC_BLOCKS = 10
WIN_BLOCKS = 16


def shifted(shard, axis, by):
    length = lax.axis_size(axis)
    pairs = [(i, i + by) for i in range(length) if 0 <= i + by < length]
    return lax.ppermute(shard, axis, pairs)


def doc_index(positions, doc_bounds):
    flat = positions.reshape(-1)
    edges = doc_bounds[1:]
    counts = jnp.sum((edges[None, :] <= flat[:, None]).astype(jnp.int32), axis=1)
    return counts.reshape(positions.shape)


def local(query, key, value, attn_out, grad_out, log_norm, doc_bounds, local_pairs, ship_table):
    position = lax.axis_index("ctx")
    tokens, features = query.shape
    kv_features = key.shape[1]
    heads = log_norm.shape[0]
    own_blocks = tokens // BLOCK
    offsets = jnp.arange(BLOCK, dtype=jnp.int32)
    own_keyval = jnp.concatenate([key, value], axis=1)
    first_used = min(max(REACH * own_blocks - DOC_BLOCKS, 0), own_blocks) * BLOCK
    pieces = [(first_used // BLOCK, shifted(own_keyval[first_used:], "ctx", REACH))]
    for hop in range(REACH - 1, 0, -1):
        pieces.append(((REACH - hop) * own_blocks, shifted(own_keyval, "ctx", hop)))
    pieces.append((REACH * own_blocks, own_keyval))
    first_block = position * own_blocks
    query_pos = (first_block + jnp.arange(own_blocks, dtype=jnp.int32))[:, None] * BLOCK + offsets
    window_first = first_block - REACH * own_blocks
    key_pos = (window_first * BLOCK + jnp.arange(WIN_BLOCKS * BLOCK, dtype=jnp.int32))
    own_ship = ship_table[position]
    ship_keys = own_ship[:, 1:]
    ship_queries = jnp.where(ship_keys >= 0, own_ship[:, :1], -1)
    ship_pairs = jnp.stack([ship_queries, ship_keys], axis=2).reshape(-1, 2)
    pairs = jnp.concatenate([local_pairs, ship_pairs], axis=0)
    grad_query, far_low, own_grads = run_pairs(
        pairs, query, grad_out, attn_out, log_norm, query_pos,
        pieces, key_pos, doc_bounds,
    )
    segments = far_low.reshape(REACH, own_blocks * BLOCK, 2 * kv_features)
    for hop in range(1, REACH):
        own_grads = own_grads + shifted(segments[REACH - hop], "ctx", -hop)
    far_grads = shifted(segments[0][first_used:], "ctx", -REACH)
    own_grads = own_grads.at[first_used:].add(far_grads.astype(jnp.float32))
    grad_key = own_grads[:, :kv_features].astype(jnp.bfloat16)
    grad_value = own_grads[:, kv_features:].astype(jnp.bfloat16)
    return (grad_query, grad_key, grad_value)


def solution(mesh):
    in_specs = (
        P("ctx", "head"),
        P("ctx", "head"),
        P("ctx", "head"),
        P("ctx", "head"),
        P("ctx", "head"),
        P("head", "ctx"),
        P(),
        P("ctx", None),
        P(),
    )
    out_specs = (P("ctx", "head"), P("ctx", "head"), P("ctx", "head"))
    return jax.shard_map(local, mesh=mesh, in_specs=in_specs, out_specs=out_specs, check_vma=False)
```

```python
import functools
import jax
import jax.numpy as jnp
from jax import lax
from jax.experimental import pallas as pl
from jax.experimental.pallas import tpu as pltpu
from jax.sharding import PartitionSpec as P

HEAD_DIM = 128
BLOCK = 128

NT = (((1,), (1,)), ((), ()))
TN = (((0,), (0,)), ((), ()))


def pair_kernel(piece_starts, pairs_ref, q_ref, do_ref, o_ref, norm_ref, qdoc_ref, qpos_ref,
                kdoc_ref, kpos_ref, *refs):
    piece_refs = refs[:len(piece_starts)]
    dq_out, far_out, own_out, delta_ref, dq_ref, dkv_ref = refs[len(piece_starts):]
    dq_ref[...] = jnp.zeros(dq_ref.shape, jnp.float32)
    dkv_ref[...] = jnp.zeros(dkv_ref.shape, jnp.float32)
    heads = norm_ref.shape[1] // BLOCK
    kv_features = piece_refs[0].shape[1] // 2
    kv_heads = kv_features // HEAD_DIM
    group = heads // kv_heads
    scale = HEAD_DIM ** (-0.5)

    def one_delta(qb, carry):
        rows = pl.ds(pl.multiple_of(qb * BLOCK, BLOCK), BLOCK)
        for h in range(heads):
            cols = pl.ds(h * HEAD_DIM, HEAD_DIM)
            prod = do_ref[rows, cols].astype(jnp.float32) * o_ref[rows, cols].astype(jnp.float32)
            delta_ref[qb, :, pl.ds(h * BLOCK, BLOCK)] = jnp.sum(prod.T, axis=0, keepdims=True)
        return carry

    lax.fori_loop(0, q_ref.shape[0] // BLOCK, one_delta, 0)

    def body(i, carry):
        qb_raw = pairs_ref[2 * i]
        kb_raw = pairs_ref[2 * i + 1]
        live = (qb_raw >= 0) & (kb_raw >= 0)
        qb = jnp.maximum(qb_raw, 0)
        kb = jnp.maximum(kb_raw, 0)
        for start, kv_ref in zip(piece_starts, piece_refs):
            end = start + kv_ref.shape[0] // BLOCK
            inside = live & (kb >= start) & (kb < end)
            pl.when(inside)(functools.partial(one_pair, qb, kb, kv_ref, start))
        return carry

    def one_pair(qb, kb, kv_ref, start):
        local_row = pl.multiple_of((kb - start) * BLOCK, BLOCK)
        qrow = pl.multiple_of(qb * BLOCK, BLOCK)
        krow = pl.multiple_of(kb * BLOCK, BLOCK)
        qdoc = qdoc_ref[pl.ds(qb, 1), :]
        qpos = qpos_ref[pl.ds(qb, 1), :]
        kdoc = kdoc_ref[pl.ds(krow, BLOCK), :]
        kpos = kpos_ref[pl.ds(krow, BLOCK), :]
        allowed = (kdoc == qdoc) & (kpos <= qpos)
        wide_allowed = jnp.concatenate([allowed] * group, axis=1)
        for g in range(kv_heads):
            k = kv_ref[pl.ds(local_row, BLOCK), pl.ds(g * HEAD_DIM, HEAD_DIM)]
            v = kv_ref[pl.ds(local_row, BLOCK), pl.ds(kv_features + g * HEAD_DIM, HEAD_DIM)]
            head_cols = [pl.ds((g * group + j) * HEAD_DIM, HEAD_DIM) for j in range(group)]
            q = jnp.concatenate([q_ref[pl.ds(qrow, BLOCK), c] for c in head_cols], axis=0)
            do = jnp.concatenate([do_ref[pl.ds(qrow, BLOCK), c] for c in head_cols], axis=0)
            group_cols = pl.ds(g * group * BLOCK, group * BLOCK)
            norm = norm_ref[pl.ds(qb, 1), group_cols]
            dl = delta_ref[qb, :, group_cols]
            scores = lax.dot_general(k, q, NT, preferred_element_type=jnp.float32) * scale
            weights = jnp.where(wide_allowed, jnp.exp(scores - norm), 0.0)
            weight_grads = lax.dot_general(v, do, NT, preferred_element_type=jnp.float32)
            score_grads = (weights * (weight_grads - dl)).astype(jnp.bfloat16)
            weights_low = weights.astype(jnp.bfloat16)
            dv = jnp.dot(weights_low, do, preferred_element_type=jnp.float32)
            dk = jnp.dot(score_grads, q, preferred_element_type=jnp.float32)
            part_query = lax.dot_general(score_grads, k, TN, preferred_element_type=jnp.float32)
            for j, c in enumerate(head_cols):
                dq_ref[pl.ds(qrow, BLOCK), c] += part_query[j * BLOCK:(j + 1) * BLOCK]
            dkv_ref[pl.ds(krow, BLOCK), pl.ds(g * HEAD_DIM, HEAD_DIM)] += dk * scale
            dkv_ref[pl.ds(krow, BLOCK), pl.ds(kv_features + g * HEAD_DIM, HEAD_DIM)] += dv

    lax.fori_loop(0, pairs_ref.shape[0] // 2, body, 0)

    def finish_query(qb, carry):
        rows = pl.ds(pl.multiple_of(qb * BLOCK, BLOCK), BLOCK)
        dq_out[rows, :] = (dq_ref[rows, :] * scale).astype(dq_out.dtype)
        return carry

    lax.fori_loop(0, dq_ref.shape[0] // BLOCK, finish_query, 0)
    far_rows = far_out.shape[0]
    far_out[...] = dkv_ref[pl.ds(0, far_rows), :].astype(far_out.dtype)
    own_out[...] = dkv_ref[pl.ds(far_rows, own_out.shape[0]), :]


def run_pairs(pairs, queries, outgrads, outputs, norms, query_pos, pieces, key_pos, doc_bounds):
    q_doc = doc_index(query_pos, doc_bounds)
    k_doc = doc_index(key_pos, doc_bounds)
    tokens, features = queries.shape
    window = key_pos.shape[0]
    both = pieces[0][1].shape[1]
    own_rows = pieces[-1][1].shape[0]
    heads = norms.shape[0]
    blocks = tokens // BLOCK
    norms = norms.reshape(heads, blocks, BLOCK).transpose(1, 0, 2).reshape(blocks, heads * BLOCK)
    vmem = pltpu.MemorySpace.VMEM
    smem = pltpu.MemorySpace.SMEM
    args = (
        pairs.reshape(-1).astype(jnp.int32),
        queries, outgrads, outputs, norms,
        q_doc, query_pos,
        k_doc.reshape(window, 1), key_pos.reshape(window, 1),
    ) + tuple(rows for _, rows in pieces)
    specs = [pl.BlockSpec(memory_space=smem)] + [pl.BlockSpec(memory_space=vmem)] * (len(args) - 1)
    kernel = functools.partial(pair_kernel, tuple(start for start, _ in pieces))
    return pl.pallas_call(
        kernel,
        out_shape=(
            jax.ShapeDtypeStruct((tokens, features), jnp.bfloat16),
            jax.ShapeDtypeStruct((window - own_rows, both), jnp.bfloat16),
            jax.ShapeDtypeStruct((own_rows, both), jnp.float32),
        ),
        in_specs=specs,
        out_specs=tuple(pl.BlockSpec(memory_space=vmem) for _ in range(3)),
        scratch_shapes=[
            pltpu.VMEM((blocks, 1, heads * BLOCK), jnp.float32),
            pltpu.VMEM((tokens, features), jnp.float32),
            pltpu.VMEM((window, both), jnp.float32),
        ],
        compiler_params=pltpu.CompilerParams(vmem_limit_bytes=48 * 1024 * 1024),
    )(*args)


REACH = 3
DOC_BLOCKS = 10
WIN_BLOCKS = 16


def shifted(shard, axis, by):
    length = lax.axis_size(axis)
    pairs = [(i, i + by) for i in range(length) if 0 <= i + by < length]
    return lax.ppermute(shard, axis, pairs)


def doc_index(positions, doc_bounds):
    flat = positions.reshape(-1)
    edges = doc_bounds[1:]
    counts = jnp.sum((edges[None, :] <= flat[:, None]).astype(jnp.int32), axis=1)
    return counts.reshape(positions.shape)


def local_body(query, key, value, attn_out, grad_out, log_norm, doc_bounds, local_pairs, ship_table):
    position = lax.axis_index("ctx")
    tokens, _ = query.shape
    kv_features = key.shape[1]
    own_blocks = tokens // BLOCK
    offsets = jnp.arange(BLOCK, dtype=jnp.int32)
    own_keyval = jnp.concatenate([key, value], axis=1)
    first_used = min(max(REACH * own_blocks - DOC_BLOCKS, 0), own_blocks) * BLOCK
    pieces = [(first_used // BLOCK, shifted(own_keyval[first_used:], "ctx", REACH))]
    for hop in range(REACH - 1, 0, -1):
        pieces.append(((REACH - hop) * own_blocks, shifted(own_keyval, "ctx", hop)))
    pieces.append((REACH * own_blocks, own_keyval))
    first_block = position * own_blocks
    query_pos = (first_block + jnp.arange(own_blocks, dtype=jnp.int32))[:, None] * BLOCK + offsets
    window_first = first_block - REACH * own_blocks
    key_pos = (window_first * BLOCK + jnp.arange(WIN_BLOCKS * BLOCK, dtype=jnp.int32))
    own_ship = ship_table[position]
    ship_keys = own_ship[:, 1:]
    ship_queries = jnp.where(ship_keys >= 0, own_ship[:, :1], -1)
    ship_pairs = jnp.stack([ship_queries, ship_keys], axis=2).reshape(-1, 2)
    pairs = jnp.concatenate([local_pairs, ship_pairs], axis=0)
    grad_query, far_low, own_grads = run_pairs(
        pairs, query, grad_out, attn_out, log_norm, query_pos,
        pieces, key_pos, doc_bounds,
    )
    segments = far_low.reshape(REACH, own_blocks * BLOCK, 2 * kv_features)
    far_grads = shifted(segments[0][first_used:], "ctx", -REACH)
    for hop in range(1, REACH):
        own_grads = own_grads + shifted(segments[REACH - hop], "ctx", -hop)
    own_grads = own_grads.at[first_used:].add(far_grads.astype(jnp.float32))
    grad_key = own_grads[:, :kv_features].astype(jnp.bfloat16)
    grad_value = own_grads[:, kv_features:].astype(jnp.bfloat16)
    return (grad_query, grad_key, grad_value)


def solution(mesh):
    in_specs = (
        P("ctx", "head"),
        P("ctx", "head"),
        P("ctx", "head"),
        P("ctx", "head"),
        P("ctx", "head"),
        P("head", "ctx"),
        P(),
        P("ctx", None),
        P(),
    )
    out_specs = (P("ctx", "head"), P("ctx", "head"), P("ctx", "head"))
    return jax.shard_map(local_body, mesh=mesh, in_specs=in_specs, out_specs=out_specs, check_vma=False)
```

```python
import functools
import jax
import jax.numpy as jnp
from jax import lax
from jax.experimental import pallas as pl
from jax.experimental.pallas import tpu as pltpu
from jax.sharding import PartitionSpec as P

HEAD_DIM = 128
BLOCK = 128

NT = (((1,), (1,)), ((), ()))
TN = (((0,), (0,)), ((), ()))


def pair_kernel(piece_starts, pairs_ref, q_ref, do_ref, o_ref, norm_ref, qdoc_ref, qpos_ref,
                kdoc_ref, kpos_ref, *refs):
    piece_refs = refs[:len(piece_starts)]
    dq_out, tail_out, far_out, own_out, delta_ref, dq_ref, dkv_ref = refs[len(piece_starts):]
    dq_ref[...] = jnp.zeros(dq_ref.shape, jnp.float32)
    dkv_ref[...] = jnp.zeros(dkv_ref.shape, jnp.float32)
    heads = norm_ref.shape[1] // BLOCK
    kv_features = piece_refs[0].shape[1] // 2
    kv_heads = kv_features // HEAD_DIM
    group = heads // kv_heads
    scale = HEAD_DIM ** (-0.5)

    def one_delta(qb, carry):
        rows = pl.ds(pl.multiple_of(qb * BLOCK, BLOCK), BLOCK)
        for h in range(heads):
            cols = pl.ds(h * HEAD_DIM, HEAD_DIM)
            prod = do_ref[rows, cols].astype(jnp.float32) * o_ref[rows, cols].astype(jnp.float32)
            delta_ref[qb, :, pl.ds(h * BLOCK, BLOCK)] = jnp.sum(prod.T, axis=0, keepdims=True)
        return carry

    lax.fori_loop(0, q_ref.shape[0] // BLOCK, one_delta, 0)

    def body(i, carry):
        qb_raw = pairs_ref[2 * i]
        kb_raw = pairs_ref[2 * i + 1]
        live = (qb_raw >= 0) & (kb_raw >= 0)
        qb = jnp.maximum(qb_raw, 0)
        kb = jnp.maximum(kb_raw, 0)
        for start, kv_ref in zip(piece_starts, piece_refs):
            end = start + kv_ref.shape[0] // BLOCK
            inside = live & (kb >= start) & (kb < end)
            pl.when(inside)(functools.partial(one_pair, qb, kb, kv_ref, start))
        return carry

    def one_pair(qb, kb, kv_ref, start):
        local_row = pl.multiple_of((kb - start) * BLOCK, BLOCK)
        qrow = pl.multiple_of(qb * BLOCK, BLOCK)
        krow = pl.multiple_of(kb * BLOCK, BLOCK)
        qdoc = qdoc_ref[pl.ds(qb, 1), :]
        qpos = qpos_ref[pl.ds(qb, 1), :]
        kdoc = kdoc_ref[pl.ds(krow, BLOCK), :]
        kpos = kpos_ref[pl.ds(krow, BLOCK), :]
        allowed = (kdoc == qdoc) & (kpos <= qpos)
        wide_allowed = jnp.concatenate([allowed] * group, axis=1)
        for g in range(kv_heads):
            k = kv_ref[pl.ds(local_row, BLOCK), pl.ds(g * HEAD_DIM, HEAD_DIM)]
            v = kv_ref[pl.ds(local_row, BLOCK), pl.ds(kv_features + g * HEAD_DIM, HEAD_DIM)]
            head_cols = [pl.ds((g * group + j) * HEAD_DIM, HEAD_DIM) for j in range(group)]
            q = jnp.concatenate([q_ref[pl.ds(qrow, BLOCK), c] for c in head_cols], axis=0)
            do = jnp.concatenate([do_ref[pl.ds(qrow, BLOCK), c] for c in head_cols], axis=0)
            group_cols = pl.ds(g * group * BLOCK, group * BLOCK)
            norm = norm_ref[pl.ds(qb, 1), group_cols]
            dl = delta_ref[qb, :, group_cols]
            scores = lax.dot_general(k, q, NT, preferred_element_type=jnp.float32) * scale
            weights = jnp.where(wide_allowed, jnp.exp(scores - norm), 0.0)
            weight_grads = lax.dot_general(v, do, NT, preferred_element_type=jnp.float32)
            score_grads = (weights * (weight_grads - dl)).astype(jnp.bfloat16)
            weights_low = weights.astype(jnp.bfloat16)
            dv = jnp.dot(weights_low, do, preferred_element_type=jnp.float32)
            dk = jnp.dot(score_grads, q, preferred_element_type=jnp.float32)
            part_query = lax.dot_general(score_grads, k, TN, preferred_element_type=jnp.float32)
            for j, c in enumerate(head_cols):
                dq_ref[pl.ds(qrow, BLOCK), c] += part_query[j * BLOCK:(j + 1) * BLOCK]
            dkv_ref[pl.ds(krow, BLOCK), pl.ds(g * HEAD_DIM, HEAD_DIM)] += dk * scale
            dkv_ref[pl.ds(krow, BLOCK), pl.ds(kv_features + g * HEAD_DIM, HEAD_DIM)] += dv

    lax.fori_loop(0, pairs_ref.shape[0] // 2, body, 0)

    def finish_query(qb, carry):
        rows = pl.ds(pl.multiple_of(qb * BLOCK, BLOCK), BLOCK)
        dq_out[rows, :] = (dq_ref[rows, :] * scale).astype(dq_out.dtype)
        return carry

    lax.fori_loop(0, dq_ref.shape[0] // BLOCK, finish_query, 0)
    near_start = piece_starts[1] * BLOCK
    tail_start = piece_starts[0] * BLOCK
    tail_out[...] = dkv_ref[pl.ds(tail_start, near_start - tail_start), :].astype(tail_out.dtype)
    far_rows = far_out.shape[0]
    far_out[...] = dkv_ref[pl.ds(near_start, far_rows), :].astype(far_out.dtype)
    own_out[...] = dkv_ref[pl.ds(near_start + far_rows, own_out.shape[0]), :]


def run_pairs(pairs, queries, outgrads, outputs, norms, query_pos, pieces, key_pos, doc_bounds):
    q_doc = doc_index(query_pos, doc_bounds)
    k_doc = doc_index(key_pos, doc_bounds)
    tokens, features = queries.shape
    window = key_pos.shape[0]
    both = pieces[0][1].shape[1]
    own_rows = pieces[-1][1].shape[0]
    heads = norms.shape[0]
    blocks = tokens // BLOCK
    norms = norms.reshape(heads, blocks, BLOCK).transpose(1, 0, 2).reshape(blocks, heads * BLOCK)
    vmem = pltpu.MemorySpace.VMEM
    smem = pltpu.MemorySpace.SMEM
    args = (
        pairs.reshape(-1).astype(jnp.int32),
        queries, outgrads, outputs, norms,
        q_doc, query_pos,
        k_doc.reshape(window, 1), key_pos.reshape(window, 1),
    ) + tuple(rows for _, rows in pieces)
    specs = [pl.BlockSpec(memory_space=smem)] + [pl.BlockSpec(memory_space=vmem)] * (len(args) - 1)
    kernel = functools.partial(pair_kernel, tuple(start for start, _ in pieces))
    return pl.pallas_call(
        kernel,
        out_shape=(
            jax.ShapeDtypeStruct((tokens, features), jnp.bfloat16),
            jax.ShapeDtypeStruct(((pieces[1][0] - pieces[0][0]) * BLOCK, both), jnp.bfloat16),
            jax.ShapeDtypeStruct((window - own_rows - pieces[1][0] * BLOCK, both), jnp.bfloat16),
            jax.ShapeDtypeStruct((own_rows, both), jnp.float32),
        ),
        in_specs=specs,
        out_specs=tuple(pl.BlockSpec(memory_space=vmem) for _ in range(4)),
        scratch_shapes=[
            pltpu.VMEM((blocks, 1, heads * BLOCK), jnp.float32),
            pltpu.VMEM((tokens, features), jnp.float32),
            pltpu.VMEM((window, both), jnp.float32),
        ],
        compiler_params=pltpu.CompilerParams(vmem_limit_bytes=48 * 1024 * 1024),
    )(*args)


REACH = 3
DOC_BLOCKS = 10
WIN_BLOCKS = 16


def shifted(shard, axis, by):
    length = lax.axis_size(axis)
    pairs = [(i, i + by) for i in range(length) if 0 <= i + by < length]
    return lax.ppermute(shard, axis, pairs)


def doc_index(positions, doc_bounds):
    flat = positions.reshape(-1)
    edges = doc_bounds[1:]
    counts = jnp.sum((edges[None, :] <= flat[:, None]).astype(jnp.int32), axis=1)
    return counts.reshape(positions.shape)


def local(query, key, value, attn_out, grad_out, log_norm, doc_bounds, local_pairs, ship_table):
    position = lax.axis_index("ctx")
    tokens, features = query.shape
    kv_features = key.shape[1]
    heads = log_norm.shape[0]
    own_blocks = tokens // BLOCK
    offsets = jnp.arange(BLOCK, dtype=jnp.int32)
    own_keyval = jnp.concatenate([key, value], axis=1)
    first_used = min(max(REACH * own_blocks - DOC_BLOCKS, 0), own_blocks) * BLOCK
    pieces = [(first_used // BLOCK, shifted(own_keyval[first_used:], "ctx", REACH))]
    for hop in range(REACH - 1, 0, -1):
        pieces.append(((REACH - hop) * own_blocks, shifted(own_keyval, "ctx", hop)))
    pieces.append((REACH * own_blocks, own_keyval))
    first_block = position * own_blocks
    query_pos = (first_block + jnp.arange(own_blocks, dtype=jnp.int32))[:, None] * BLOCK + offsets
    window_first = first_block - REACH * own_blocks
    key_pos = (window_first * BLOCK + jnp.arange(WIN_BLOCKS * BLOCK, dtype=jnp.int32))
    own_ship = ship_table[position]
    ship_keys = own_ship[:, 1:]
    ship_queries = jnp.where(ship_keys >= 0, own_ship[:, :1], -1)
    ship_pairs = jnp.stack([ship_queries, ship_keys], axis=2).reshape(-1, 2)
    pairs = jnp.concatenate([local_pairs, ship_pairs], axis=0)
    grad_query, tail_low, far_low, own_grads = run_pairs(
        pairs, query, grad_out, attn_out, log_norm, query_pos,
        pieces, key_pos, doc_bounds,
    )
    segments = far_low.reshape(REACH - 1, own_blocks * BLOCK, 2 * kv_features)
    for hop in range(1, REACH):
        own_grads = own_grads + shifted(segments[REACH - 1 - hop], "ctx", -hop)
    far_grads = shifted(tail_low, "ctx", -REACH)
    own_grads = own_grads.at[first_used:].add(far_grads.astype(jnp.float32))
    grad_key = own_grads[:, :kv_features].astype(jnp.bfloat16)
    grad_value = own_grads[:, kv_features:].astype(jnp.bfloat16)
    return (grad_query, grad_key, grad_value)


def solution(mesh):
    in_specs = (
        P("ctx", "head"),
        P("ctx", "head"),
        P("ctx", "head"),
        P("ctx", "head"),
        P("ctx", "head"),
        P("head", "ctx"),
        P(),
        P("ctx", None),
        P(),
    )
    out_specs = (P("ctx", "head"), P("ctx", "head"), P("ctx", "head"))
    return jax.shard_map(local, mesh=mesh, in_specs=in_specs, out_specs=out_specs, check_vma=False)
```
